512 devices in a mesh: spec: 16 (over z_hi, y, core), neuron: 32 (over x, z_lo).
Axes of the slice: x: 4, y: 4, z: 16 (z_hi: 2, z_lo: 8; z = z_hi * 8 + z_lo), core: 2. Of those that a mesh axis runs over, the one named last changes fastest.
Arguments:
- class_scores: bfloat16 [384, 10, 32768], P('spec', None, 'neuron'), may hold values from -6 to 6
- true_class: int32 [384], P('spec'), may hold values from 0 to 9
- weight_blocks: bfloat16 [512, 64, 2048], P('neuron'), may hold values from -0.125 to 0.125
- col_blocks: int32 [512, 32], P('neuron'), may hold values from 0 to 511, as said below
- layer_bias: bfloat16 [32768], P('neuron'), may hold values from -0.119628906 to 0.119628906
- bound_mid: float32 [32768], P('neuron'), may hold values from -6 to 6
- bound_rad: float32 [32768], P('neuron'), may hold values from 0.05 to 2
- lower_slope: float32 [32768], P('neuron'), may hold values from 0 to 1
- unstable_blocks: int32 [512], P('neuron'), may hold values 0 or 1
Outputs:
- coefficients: bfloat16 [384, 9, 32768], P('spec', None, 'neuron')
- offsets: float32 [384, 9], P('spec')
The draws below stay inside these ranges and needn't reach their ends.
Inputs may be any that keep to these rules, and one draw needn't show every extreme that they name: `col_blocks`: the 32 entries of a row r are distinct and name blocks of input neurons owned by the neuron index r // 16 or by its two neighbours on the closed loop of 32 indices.
All inputs are finite; a program needn't handle non-finite values. No bound on the sum of `unstable_blocks` on one device may be relied on, other than what follows from the above.
Results may differ from the reference program's by a relative error of at most 0.001.
The reference program's roundings to bfloat16 on the way (of `margin`) count: a program that leaves them out, or rounds other values in their place, can miss the bound.
Values sent between devices are 32-bit elements; how exact they have to be, the bound alone decides.
No kernel may reach another device: no remote copies, remote signals or barrier semaphores. Data moves between devices by JAX's collectives and lax.ppermute only.
A program may use at most 64 MiB of HBM per device.

```python
import math
import jax
import jax.numpy as jnp
from jax import lax

N = 32768
BS = 64
K = 32
CLASSES = 10
SPECS = 9
SAMPLES = 384
NB = 512
BPD = 16


def draw_col_blocks(key, part):
    span = 3 * BPD
    scores = jax.random.randint(key, (NB, span), 0, 2 ** 20) * span + jnp.arange(span, dtype=jnp.int32)[None, :]
    offsets = jnp.argsort(scores, axis=1)[:, :K].astype(jnp.int32)
    owner = jnp.arange(NB, dtype=jnp.int32) // BPD
    return ((owner[:, None] - 1) * BPD + offsets) % NB


def plant(drawn, stream_key, smallest, high):
    extent = drawn.shape
    index_at = [jax.random.randint(jax.random.fold_in(stream_key, axis), (), 0, extent[axis]) for axis in range(len(extent))]
    drawn = drawn.at[tuple(index_at)].set(smallest)
    longest = extent.index(max(extent))
    index_at[longest] = (index_at[longest] + 1) % extent[longest]
    return drawn.at[tuple(index_at)].set(high)


def block_scale(stream_key, shape, split, smallest, largest):
    level = 1.0
    for dim, parts in split:
        steps = jax.random.uniform(jax.random.fold_in(jax.random.fold_in(stream_key, 6), dim), (parts,), jnp.float32, smallest / len(split), largest / len(split))
        level = level * jnp.repeat(jnp.exp(steps), shape[dim] // parts).reshape((-1,) + (1,) * (len(shape) - 1 - dim))
    return level


def scatter_about(key, shape, width, limit, shards=(), kind=jnp.bfloat16):
    factor_of = block_scale(key, shape, shards, -0.22, 0.18) if shards else 1.0
    result = jax.random.normal(key, shape, jnp.float32) * width * factor_of
    return jnp.minimum(jnp.maximum(result, -limit), limit).astype(kind)


def setup_inputs(seed: int = 0) -> dict:
    key_of = jax.random.split(jax.random.key(seed), 10)
    return {
        "class_scores": scatter_about(key_of[0], (SAMPLES, CLASSES, N), 1.0, 6.0, ((0, 16), (2, 32))),
        "true_class": plant(jax.random.randint(key_of[1], (SAMPLES,), 0, CLASSES), jax.random.fold_in(key_of[1], 1), 0, CLASSES - 1).astype(jnp.int32),
        "weight_blocks": scatter_about(key_of[2], (NB, BS, K * BS), (K * BS) ** -0.5, 0.125, ((0, 32),)),
        "col_blocks": draw_col_blocks(jax.random.fold_in(key_of[9], 71), 0),
        "layer_bias": scatter_about(key_of[4], (N,), 0.02, 0.119628906, ((0, 32),)),
        "bound_mid": scatter_about(key_of[5], (N,), 1.0, 6.0, ((0, 32),), jnp.float32),
        "bound_rad": jnp.clip(jnp.exp(math.log(2.0) - 3.6888794 * jax.random.uniform(key_of[6], (N,), jnp.float32) ** block_scale(key_of[6], (N,), ((0, 32),), -0.2, 0.2)), 0.05, 2.0),
        "lower_slope": jnp.clip(1.0 * jax.random.uniform(key_of[7], (N,), jnp.float32) ** block_scale(key_of[7], (N,), ((0, 32),), -0.2, 0.2), 0.0, 1.0),
        "unstable_blocks": plant((jax.random.randint(key_of[8], (NB,), 0, 3) < 1).astype(jnp.int32), jax.random.fold_in(key_of[8], 1), 0, 1),
    }


def reference(class_scores, true_class, weight_blocks, col_blocks, layer_bias, bound_mid, bound_rad, lower_slope, unstable_blocks):
    labels = true_class.astype(jnp.int32)
    spec_ids = jnp.arange(SPECS, dtype=jnp.int32)
    others = spec_ids[None, :] + (spec_ids[None, :] >= labels[:, None]).astype(jnp.int32)
    top = jnp.take_along_axis(class_scores, labels[:, None, None], axis=1).astype(jnp.float32)
    rest = jnp.take_along_axis(class_scores, others[:, :, None], axis=1).astype(jnp.float32)
    margin = (top - rest).astype(jnp.bfloat16)
    total_rows = SAMPLES * SPECS
    flat = margin.reshape(total_rows, NB, BS)

    def add_row(r, acc):
        left = lax.dynamic_index_in_dim(flat, r, 1, keepdims=False)
        block_w = lax.dynamic_index_in_dim(weight_blocks, r, 0, keepdims=False)
        contrib = jnp.dot(left, block_w, preferred_element_type=jnp.float32).reshape(total_rows, K, BS)
        targets = lax.dynamic_index_in_dim(col_blocks, r, 0, keepdims=False).astype(jnp.int32)
        return acc.at[:, targets].add(contrib)

    propagated = lax.fori_loop(0, NB, add_row, jnp.zeros((total_rows, NB, BS), jnp.float32))
    propagated = propagated.reshape(total_rows, N)
    lower = bound_mid - bound_rad
    upper = bound_mid + bound_rad
    up_slope = (jax.nn.relu(upper) - jax.nn.relu(lower)) / (upper - lower)
    up_shift = jax.nn.relu(lower) - up_slope * lower
    flags = jnp.repeat(unstable_blocks, BS)
    low_slope = jnp.where(flags == 1, lower_slope, up_slope)
    negative = jnp.minimum(propagated, 0.0)
    coefficients = (low_slope * jnp.maximum(propagated, 0.0) + up_slope * negative).astype(jnp.bfloat16)
    offsets = jnp.dot(margin.reshape(total_rows, N), layer_bias, preferred_element_type=jnp.float32)
    offsets = offsets + jnp.dot(negative, up_shift, precision=lax.Precision.HIGHEST)
    return coefficients.reshape(SAMPLES, SPECS, N), offsets.reshape(SAMPLES, SPECS)
```

```python
import jax
import jax.numpy as jnp
from jax import lax
from jax.experimental import pallas as pl
from jax.experimental.pallas import tpu as pltpu
from jax.sharding import PartitionSpec as P

LANES = 128


def shift_by(value, axis, by):
    length = lax.axis_size(axis)
    return lax.ppermute(value, axis, [(i, (i + by) % length) for i in range(length)])


def products_kernel(
    base_ref,
    label_ref,
    cols_ref,
    scores_ref,
    bias_ref,
    weights_hbm,
    down_ref,
    centre_ref,
    up_ref,
    bias_acc_ref,
    tiles_ref,
    spread_ref,
    margin_ref,
    codes_ref,
    codes_smem,
    code_sem,
    sems,
):
    block_rows, blocksize, packed = weights_hbm.shape
    kept = packed // blocksize
    source_tiles = packed // LANES
    turned_at = source_tiles + 1
    classes, samples, width = scores_ref.shape
    specs = classes - 1
    chunks = sems.shape[0]
    per_chunk = block_rows // chunks
    copies = [
        pltpu.make_async_copy(
            weights_hbm.at[pl.ds(c * per_chunk, per_chunk)],
            tiles_ref.at[pl.ds(c * per_chunk, per_chunk), :, pl.ds(0, packed)],
            sems.at[c],
        )
        for c in range(chunks)
    ]
    for copy in copies:
        copy.start()

    total_blocks = lax.axis_size("neuron") * block_rows
    positions = (cols_ref[...] - base_ref[0]) & (total_blocks - 1)
    slot = lax.broadcasted_iota(jnp.int32, (block_rows, LANES), 1)
    found = jnp.full((block_rows, LANES), -1, jnp.int32)
    for k in range(kept):
        found = jnp.where(slot == positions[:, k : k + 1], k, found)
    same_half = (found & 1) == (slot & 1)
    tile = found >> 1
    codes = jnp.where(found < 0, source_tiles, jnp.where(same_half, tile, tile + turned_at))
    codes_ref[...] = codes
    code_copy = pltpu.make_async_copy(codes_ref, codes_smem, code_sem)
    code_copy.start()

    row = lax.broadcasted_iota(jnp.int32, (samples, width), 0)
    labels = jnp.zeros((samples, width), jnp.int32)
    for s in range(samples):
        labels = jnp.where(row == s, label_ref[s], labels)
    scores = [scores_ref[c].astype(jnp.float32) for c in range(classes)]
    top = scores[0]
    for c in range(1, classes):
        top = jnp.where(labels == c, scores[c], top)
    bias = bias_ref[...].astype(jnp.float32)
    for j in range(specs):
        rest = jnp.where(labels > j, scores[j], scores[j + 1])
        margin = (top - rest).astype(jnp.bfloat16)
        margin_ref[pl.ds(j * samples, samples), :] = margin
        terms = margin.astype(jnp.float32) * bias
        acc = terms[:, :LANES]
        for t in range(1, width // LANES):
            acc = acc + terms[:, t * LANES : (t + 1) * LANES]
        bias_acc_ref[pl.ds(j * samples, samples), :] = acc

    tiles_ref[:, :, packed : packed + LANES] = jnp.zeros((block_rows, blocksize, LANES), jnp.bfloat16)
    low_half = lax.broadcasted_iota(jnp.int32, (blocksize, LANES), 1) < blocksize
    code_copy.wait()

    for c in range(chunks):
        copies[c].wait()

        def place(i, carry):
            r = c * per_chunk + i
            first = pl.multiple_of(r * blocksize, blocksize)
            for t in range(source_tiles):
                source = tiles_ref[r, :, t * LANES : (t + 1) * LANES]
                at = (turned_at + t) * LANES
                tiles_ref[r, :, at : at + LANES] = pltpu.roll(source, blocksize, 1)
            for q in range(3 * width // LANES):
                left = pl.multiple_of(codes_smem[r, 2 * q] * LANES, LANES)
                right = pl.multiple_of(codes_smem[r, 2 * q + 1] * LANES, LANES)
                spread_ref[pl.ds(first, blocksize), q * LANES : (q + 1) * LANES] = jnp.where(
                    low_half, tiles_ref[r, :, pl.ds(left, LANES)], tiles_ref[r, :, pl.ds(right, LANES)]
                )
            return carry

        lax.fori_loop(0, per_chunk, place, 0)

    step = 256
    for part, out in ((0, down_ref), (2, up_ref), (1, centre_ref)):
        for t in range(width // step):
            at = part * width + t * step
            out[:, t * step : (t + 1) * step] = jnp.dot(
                margin_ref[...], spread_ref[:, at : at + step], preferred_element_type=jnp.float32
            )


def products(base, labels, cols, scores, bias, weights):
    classes, samples, width = scores.shape
    rows = (classes - 1) * samples
    block_rows, blocksize, packed = weights.shape
    part = jax.ShapeDtypeStruct((rows, width), jnp.float32)
    smem = pl.BlockSpec(memory_space=pltpu.SMEM)
    vmem = pl.BlockSpec(memory_space=pltpu.VMEM)
    return pl.pallas_call(
        products_kernel,
        out_shape=(part, part, part, jax.ShapeDtypeStruct((rows, LANES), jnp.float32)),
        in_specs=[smem, smem, vmem, vmem, vmem, pl.BlockSpec(memory_space=pl.ANY)],
        out_specs=(vmem, vmem, vmem, vmem),
        scratch_shapes=[
            pltpu.VMEM((block_rows, blocksize, 2 * packed + LANES), jnp.bfloat16),
            pltpu.VMEM((block_rows * blocksize, 3 * width), jnp.bfloat16),
            pltpu.VMEM((rows, width), jnp.bfloat16),
            pltpu.VMEM((block_rows, LANES), jnp.int32),
            pltpu.SMEM((block_rows, LANES), jnp.int32),
            pltpu.SemaphoreType.DMA,
            pltpu.SemaphoreType.DMA((4,)),
        ],
        compiler_params=pltpu.CompilerParams(vmem_limit_bytes=40 << 20),
        name="products",
    )(base, labels, cols, scores, bias, weights)


def relax_kernel(
    flags_ref,
    mid_ref,
    rad_ref,
    slope_ref,
    bias_acc_ref,
    centre_ref,
    higher_ref,
    lower_ref,
    coef_ref,
    offs_ref,
    acc_ref,
):
    step = pl.program_id(0)
    per_step, samples, width = coef_ref.shape
    rows = per_step * samples
    blocksize = width // flags_ref.shape[0]
    lower = mid_ref[...] - rad_ref[...]
    upper = mid_ref[...] + rad_ref[...]
    up_slope = (jnp.maximum(upper, 0.0) - jnp.maximum(lower, 0.0)) / (upper - lower)
    up_shift = jnp.maximum(lower, 0.0) - up_slope * lower
    block = lax.broadcasted_iota(jnp.int32, (1, width), 1) // blocksize
    flags = jnp.zeros((1, width), jnp.int32)
    for b in range(flags_ref.shape[0]):
        flags = jnp.where(block == b, flags_ref[b], flags)
    low_slope = jnp.where(flags == 1, slope_ref[...], up_slope)
    propagated = centre_ref[...] + higher_ref[...] + lower_ref[...]
    negative = jnp.minimum(propagated, 0.0)
    coef = (low_slope * jnp.maximum(propagated, 0.0) + up_slope * negative).astype(jnp.bfloat16)
    for j in range(per_step):
        coef_ref[j] = coef[j * samples : (j + 1) * samples]
    terms = negative * up_shift
    acc = bias_acc_ref[...]
    for t in range(width // LANES):
        acc = acc + terms[:, t * LANES : (t + 1) * LANES]
    acc_ref[pl.ds(pl.multiple_of(step * rows, 8), rows), :] = acc

    @pl.when(step == pl.num_programs(0) - 1)
    def _():
        ones = jnp.ones((8, LANES), jnp.float32)
        sums = lax.dot_general(
            ones,
            acc_ref[...],
            (((1,), (1,)), ((), ())),
            precision=lax.Precision.HIGHEST,
            preferred_element_type=jnp.float32,
        )
        for d in range(offs_ref.shape[0]):
            offs_ref[d] = sums[:1]


def relax(flags, mid, rad, slope, bias_acc, centre, higher, lower, samples, devices):
    rows, width = centre.shape
    specs = rows // samples
    steps = 3
    per_step = specs // steps
    smem = pl.BlockSpec(memory_space=pltpu.SMEM)
    vector = pl.BlockSpec((1, width), lambda i: (0, 0))
    part = pl.BlockSpec((rows // steps, width), lambda i: (i, 0))
    return pl.pallas_call(
        relax_kernel,
        grid=(steps,),
        out_shape=(
            jax.ShapeDtypeStruct((specs, samples, width), jnp.bfloat16),
            jax.ShapeDtypeStruct((devices, 1, rows), jnp.float32),
        ),
        in_specs=[
            smem,
            vector,
            vector,
            vector,
            pl.BlockSpec((rows // steps, LANES), lambda i: (i, 0)),
            part,
            part,
            part,
        ],
        out_specs=(
            pl.BlockSpec((per_step, samples, width), lambda i: (i, 0, 0)),
            pl.BlockSpec((devices, 1, rows), lambda i: (0, 0, 0)),
        ),
        scratch_shapes=[pltpu.VMEM((rows, LANES), jnp.float32)],
        name="relax",
    )(flags, mid, rad, slope, bias_acc, centre, higher, lower)


def total_kernel(parts_ref, out_ref):
    specs, samples = out_ref.shape
    sums = parts_ref[0]
    for d in range(1, parts_ref.shape[0]):
        sums = sums + parts_ref[d]
    for j in range(specs):
        out_ref[j : j + 1, :] = sums[:, j * samples : (j + 1) * samples]


def local(
    class_scores,
    true_class,
    weight_blocks,
    col_blocks,
    layer_bias,
    bound_mid,
    bound_rad,
    lower_slope,
    unstable_blocks,
):
    samples, classes, width = class_scores.shape
    specs = classes - 1
    per_dev = col_blocks.shape[0]
    devices = lax.axis_size("neuron")
    base = ((lax.axis_index("neuron") - 1) * per_dev).astype(jnp.int32).reshape(1)
    down, centre, up, bias_acc = products(
        base,
        true_class,
        col_blocks,
        jnp.transpose(class_scores, (1, 0, 2)),
        layer_bias.reshape(1, width),
        weight_blocks,
    )
    higher = shift_by(down, "neuron", -1)
    lower = shift_by(up, "neuron", 1)
    coef, offs = relax(
        unstable_blocks,
        bound_mid.reshape(1, width),
        bound_rad.reshape(1, width),
        lower_slope.reshape(1, width),
        bias_acc,
        centre,
        higher,
        lower,
        samples,
        devices,
    )
    gathered = lax.all_to_all(offs, "neuron", 0, 0)
    offsets = pl.pallas_call(
        total_kernel,
        out_shape=jax.ShapeDtypeStruct((specs, samples), jnp.float32),
        name="total",
    )(gathered)
    return jnp.transpose(coef, (1, 0, 2)), offsets.T


def solution(mesh):
    placed = (
        P("spec", None, "neuron"),
        P("spec"),
        P("neuron", None, None),
        P("neuron", None),
        P("neuron"),
        P("neuron"),
        P("neuron"),
        P("neuron"),
        P("neuron"),
    )
    return jax.shard_map(
        local,
        mesh=mesh,
        in_specs=placed,
        out_specs=(P("spec", None, "neuron"), P("spec", None)),
        check_vma=False,
    )
```

```python
import functools

import jax
import jax.numpy as jnp
from jax import lax
from jax.experimental import pallas as pl
from jax.experimental.pallas import tpu as pltpu
from jax.sharding import PartitionSpec as P

LANES = 128
CHUNKS = 4


def shift_by(value, axis, by):
    length = lax.axis_size(axis)
    return lax.ppermute(value, axis, [(i, (i + by) % length) for i in range(length)])


def start_weights(weights_hbm, tiles_ref, sems):
    packed = weights_hbm.shape[2]
    per_chunk = weights_hbm.shape[0] // CHUNKS
    copies = [
        pltpu.make_async_copy(
            weights_hbm.at[pl.ds(c * per_chunk, per_chunk)],
            tiles_ref.at[pl.ds(c * per_chunk, per_chunk), :, pl.ds(0, packed)],
            sems.at[c],
        )
        for c in range(CHUNKS)
    ]
    for copy in copies:
        copy.start()
    return copies


def make_codes(cols, base, total_blocks, source_tiles):
    block_rows, kept = cols.shape
    positions = (cols - base) & (total_blocks - 1)
    slot = lax.broadcasted_iota(jnp.int32, (block_rows, LANES), 1)
    found = jnp.full((block_rows, LANES), -1, jnp.int32)
    for k in range(kept):
        found = jnp.where(slot == positions[:, k : k + 1], k, found)
    same_half = (found & 1) == (slot & 1)
    tile = found >> 1
    return jnp.where(found < 0, source_tiles, jnp.where(same_half, tile, tile + source_tiles + 1))


def place_and_multiply(tiles_ref, spread_ref, codes_smem, margin_ref, copies, parts, outs):
    block_rows, blocksize, lanes = tiles_ref.shape
    source_tiles = (lanes // LANES - 1) // 2
    turned_at = source_tiles + 1
    per_chunk = block_rows // CHUNKS
    width = margin_ref.shape[1]
    empty = slice(source_tiles * LANES, turned_at * LANES)
    tiles_ref[:, :, empty] = jnp.zeros((block_rows, blocksize, LANES), jnp.bfloat16)
    low_half = lax.broadcasted_iota(jnp.int32, (blocksize, LANES), 1) < blocksize
    per_part = width // LANES
    for c in range(CHUNKS):
        copies[c].wait()

        def place(i, carry):
            r = c * per_chunk + i
            first = pl.multiple_of(r * blocksize, blocksize)
            for t in range(source_tiles):
                at = (turned_at + t) * LANES
                tiles_ref[r, :, at : at + LANES] = pltpu.roll(
                    tiles_ref[r, :, t * LANES : (t + 1) * LANES], blocksize, 1
                )
            for n, part in enumerate(parts):
                for q in range(per_part):
                    at = 2 * (part * per_part + q)
                    left = pl.multiple_of(codes_smem[r, at] * LANES, LANES)
                    right = pl.multiple_of(codes_smem[r, at + 1] * LANES, LANES)
                    to = n * width + q * LANES
                    spread_ref[pl.ds(first, blocksize), to : to + LANES] = jnp.where(
                        low_half,
                        tiles_ref[r, :, pl.ds(left, LANES)],
                        tiles_ref[r, :, pl.ds(right, LANES)],
                    )
            return carry

        lax.fori_loop(0, per_chunk, place, 0)
    step = 256
    for n, out in enumerate(outs):
        for t in range(width // step):
            at = n * width + t * step
            out[:, t * step : (t + 1) * step] = jnp.dot(
                margin_ref[...], spread_ref[:, at : at + step], preferred_element_type=jnp.float32
            )


def first_kernel(
    total_blocks,
    base_ref,
    labels_hbm,
    cols_hbm,
    scores_hbm,
    weights_hbm,
    down_ref,
    margin_ref,
    codes_ref,
    labels_ref,
    cols_ref,
    scores_ref,
    tiles_ref,
    spread_ref,
    codes_smem,
    small_sems,
    sems,
):
    cols_copy = pltpu.make_async_copy(cols_hbm, cols_ref, small_sems.at[0])
    labels_copy = pltpu.make_async_copy(labels_hbm, labels_ref, small_sems.at[1])
    scores_copy = pltpu.make_async_copy(scores_hbm, scores_ref, small_sems.at[2])
    cols_copy.start()
    labels_copy.start()
    scores_copy.start()
    copies = start_weights(weights_hbm, tiles_ref, sems)
    block_rows, blocksize, packed = weights_hbm.shape
    classes, samples, width = scores_ref.shape
    cols_copy.wait()
    codes_ref[...] = make_codes(
        cols_ref[...], base_ref[0], total_blocks, packed // LANES
    )
    codes_copy = pltpu.make_async_copy(codes_ref, codes_smem, small_sems.at[3])
    codes_copy.start()
    labels_copy.wait()
    row = lax.broadcasted_iota(jnp.int32, (samples, width), 0)
    labels = jnp.zeros((samples, width), jnp.int32)
    for s in range(samples):
        labels = jnp.where(row == s, labels_ref[s], labels)
    scores_copy.wait()
    scores = [scores_ref[c].astype(jnp.float32) for c in range(classes)]
    top = scores[0]
    for c in range(1, classes):
        top = jnp.where(labels == c, scores[c], top)
    for j in range(classes - 1):
        rest = jnp.where(labels > j, scores[j], scores[j + 1])
        margin_ref[pl.ds(j * samples, samples), :] = (top - rest).astype(jnp.bfloat16)
    codes_copy.wait()
    place_and_multiply(tiles_ref, spread_ref, codes_smem, margin_ref, copies, (0,), (down_ref,))


def first(total_blocks, base, labels, cols, scores, weights):
    classes, samples, width = scores.shape
    rows = (classes - 1) * samples
    block_rows, blocksize, packed = weights.shape
    hbm = pl.BlockSpec(memory_space=pltpu.HBM)
    vmem = pl.BlockSpec(memory_space=pltpu.VMEM)
    return pl.pallas_call(
        functools.partial(first_kernel, total_blocks),
        out_shape=(
            jax.ShapeDtypeStruct((rows, width), jnp.float32),
            jax.ShapeDtypeStruct((rows, width), jnp.bfloat16),
            jax.ShapeDtypeStruct((block_rows, LANES), jnp.int32),
        ),
        in_specs=[pl.BlockSpec(memory_space=pltpu.SMEM), hbm, hbm, hbm, hbm],
        out_specs=(vmem, vmem, vmem),
        scratch_shapes=[
            pltpu.SMEM((samples,), jnp.int32),
            pltpu.VMEM(cols.shape, jnp.int32),
            pltpu.VMEM(scores.shape, jnp.bfloat16),
            pltpu.VMEM((block_rows, blocksize, 2 * packed + LANES), jnp.bfloat16),
            pltpu.VMEM((block_rows * blocksize, width), jnp.bfloat16),
            pltpu.SMEM((block_rows, LANES), jnp.int32),
            pltpu.SemaphoreType.DMA((4,)),
            pltpu.SemaphoreType.DMA((CHUNKS,)),
        ],
        compiler_params=pltpu.CompilerParams(vmem_limit_bytes=61 << 20),
        cost_estimate=pl.CostEstimate(
            flops=2 * rows * width * width, bytes_accessed=6 << 20, transcendentals=0
        ),
        name="first",
    )(base, labels, cols, scores, weights)


def second_kernel(
    codes_hbm, bias_ref, margin_ref, weights_hbm, up_ref, centre_ref, bias_acc_ref, tiles_ref, spread_ref, codes_smem, small_sems, sems
):
    codes_copy = pltpu.make_async_copy(codes_hbm, codes_smem, small_sems.at[0])
    codes_copy.start()
    copies = start_weights(weights_hbm, tiles_ref, sems)
    width = margin_ref.shape[1]
    terms = margin_ref[...].astype(jnp.float32) * bias_ref[...]
    acc = terms[:, :LANES]
    for t in range(1, width // LANES):
        acc = acc + terms[:, t * LANES : (t + 1) * LANES]
    bias_acc_ref[...] = acc
    codes_copy.wait()
    place_and_multiply(tiles_ref, spread_ref, codes_smem, margin_ref, copies, (2, 1), (up_ref, centre_ref))


def second(codes, bias, margin, weights):
    rows, width = margin.shape
    block_rows, blocksize, packed = weights.shape
    hbm = pl.BlockSpec(memory_space=pltpu.HBM)
    vmem = pl.BlockSpec(memory_space=pltpu.VMEM)
    part = jax.ShapeDtypeStruct((rows, width), jnp.float32)
    return pl.pallas_call(
        second_kernel,
        out_shape=(part, part, jax.ShapeDtypeStruct((rows, LANES), jnp.float32)),
        in_specs=[vmem, vmem, vmem, hbm],
        out_specs=(vmem, vmem, vmem),
        scratch_shapes=[
            pltpu.VMEM((block_rows, blocksize, 2 * packed + LANES), jnp.bfloat16),
            pltpu.VMEM((block_rows * blocksize, 2 * width), jnp.bfloat16),
            pltpu.SMEM((block_rows, LANES), jnp.int32),
            pltpu.SemaphoreType.DMA((1,)),
            pltpu.SemaphoreType.DMA((CHUNKS,)),
        ],
        compiler_params=pltpu.CompilerParams(vmem_limit_bytes=30 << 20),
        cost_estimate=pl.CostEstimate(
            flops=4 * rows * width * width, bytes_accessed=6 << 20, transcendentals=0
        ),
        name="second",
    )(codes, bias, margin, weights)


def relax_kernel(
    flags_ref,
    mid_ref,
    rad_ref,
    slope_ref,
    bias_acc_ref,
    centre_ref,
    higher_ref,
    lower_ref,
    coef_ref,
    offs_ref,
    acc_ref,
):
    specs, samples, width = coef_ref.shape
    blocksize = width // flags_ref.shape[0]
    lower = mid_ref[...] - rad_ref[...]
    upper = mid_ref[...] + rad_ref[...]
    up_slope = (jnp.maximum(upper, 0.0) - jnp.maximum(lower, 0.0)) / (upper - lower)
    up_shift = jnp.maximum(lower, 0.0) - up_slope * lower
    block = lax.broadcasted_iota(jnp.int32, (1, width), 1) // blocksize
    flags = jnp.zeros((1, width), jnp.int32)
    for b in range(flags_ref.shape[0]):
        flags = jnp.where(block == b, flags_ref[b], flags)
    low_slope = jnp.where(flags == 1, slope_ref[...], up_slope)
    for j in range(specs):
        at = slice(j * samples, (j + 1) * samples)
        propagated = centre_ref[at] + higher_ref[at] + lower_ref[at]
        negative = jnp.minimum(propagated, 0.0)
        coef_ref[j] = (low_slope * jnp.maximum(propagated, 0.0) + up_slope * negative).astype(jnp.bfloat16)
        terms = negative * up_shift
        acc = bias_acc_ref[at]
        for t in range(width // LANES):
            acc = acc + terms[:, t * LANES : (t + 1) * LANES]
        acc_ref[at] = acc
    sums = lax.dot_general(
        jnp.ones((8, LANES), jnp.float32),
        acc_ref[...],
        (((1,), (1,)), ((), ())),
        precision=lax.Precision.HIGHEST,
        preferred_element_type=jnp.float32,
    )
    for d in range(offs_ref.shape[0]):
        offs_ref[d] = sums[:1]


def relax(flags, mid, rad, slope, bias_acc, centre, higher, lower, samples, devices):
    rows, width = centre.shape
    specs = rows // samples
    smem = pl.BlockSpec(memory_space=pltpu.SMEM)
    vmem = pl.BlockSpec(memory_space=pltpu.VMEM)
    return pl.pallas_call(
        relax_kernel,
        out_shape=(
            jax.ShapeDtypeStruct((specs, samples, width), jnp.bfloat16),
            jax.ShapeDtypeStruct((devices, 1, rows), jnp.float32),
        ),
        in_specs=[smem] + [vmem] * 7,
        out_specs=(vmem, vmem),
        scratch_shapes=[pltpu.VMEM((rows, LANES), jnp.float32)],
        compiler_params=pltpu.CompilerParams(vmem_limit_bytes=16 << 20),
        cost_estimate=pl.CostEstimate(
            flops=10 * rows * width, bytes_accessed=4 << 20, transcendentals=0
        ),
        name="relax",
    )(flags, mid, rad, slope, bias_acc, centre, higher, lower)


def total_kernel(parts_ref, out_ref):
    specs, samples = out_ref.shape
    sums = parts_ref[0]
    for d in range(1, parts_ref.shape[0]):
        sums = sums + parts_ref[d]
    for j in range(specs):
        out_ref[j : j + 1, :] = sums[:, j * samples : (j + 1) * samples]


def local(
    class_scores,
    true_class,
    weight_blocks,
    col_blocks,
    layer_bias,
    bound_mid,
    bound_rad,
    lower_slope,
    unstable_blocks,
):
    samples, classes, width = class_scores.shape
    specs = classes - 1
    per_dev = col_blocks.shape[0]
    devices = lax.axis_size("neuron")
    base = ((lax.axis_index("neuron") - 1) * per_dev).astype(jnp.int32).reshape(1)
    down, margin, codes = first(
        devices * per_dev,
        base, true_class, col_blocks, jnp.transpose(class_scores, (1, 0, 2)), weight_blocks
    )
    higher = shift_by(down, "neuron", -1)
    layer_bias, margin = lax.optimization_barrier((layer_bias, margin))
    bias = layer_bias.astype(jnp.float32).reshape(1, width)
    up, centre, bias_acc = second(codes, bias, margin, weight_blocks)
    lower = shift_by(up, "neuron", 1)
    coef, offs = relax(
        unstable_blocks,
        bound_mid.reshape(1, width),
        bound_rad.reshape(1, width),
        lower_slope.reshape(1, width),
        bias_acc,
        centre,
        higher,
        lower,
        samples,
        devices,
    )
    gathered = lax.all_to_all(offs, "neuron", 0, 0)
    offsets = pl.pallas_call(
        total_kernel,
        out_shape=jax.ShapeDtypeStruct((specs, samples), jnp.float32),
        name="total",
    )(gathered)
    return jnp.transpose(coef, (1, 0, 2)), offsets.T


def solution(mesh):
    placed = (
        P("spec", None, "neuron"),
        P("spec"),
        P("neuron", None, None),
        P("neuron", None),
        P("neuron"),
        P("neuron"),
        P("neuron"),
        P("neuron"),
        P("neuron"),
    )
    return jax.shard_map(
        local,
        mesh=mesh,
        in_specs=placed,
        out_specs=(P("spec", None, "neuron"), P("spec", None)),
        check_vma=False,
    )
```

```python
import functools

import jax
import jax.numpy as jnp
from jax import lax
from jax.experimental import pallas as pl
from jax.experimental.pallas import tpu as pltpu
from jax.sharding import PartitionSpec as P


LANES = 128
CHUNKS = 2


RUN = 8


def send(value, pairs):
    return lax.ppermute(value, "neuron", pairs)


def start_weights(weights_hbm, tiles_ref, sems):
    packed = weights_hbm.shape[2]
    per_chunk = weights_hbm.shape[0] // CHUNKS
    copies = [
        pltpu.make_async_copy(
            weights_hbm.at[pl.ds(c * per_chunk, per_chunk)],
            tiles_ref.at[pl.ds(c * per_chunk, per_chunk), :, pl.ds(0, packed)],
            sems.at[c],
        )
        for c in range(CHUNKS)
    ]
    for copy in copies:
        copy.start()
    return copies


def make_codes(cols, base, total_blocks, source_tiles):
    block_rows, kept = cols.shape
    positions = (cols - base) & (total_blocks - 1)
    slot = lax.broadcasted_iota(jnp.int32, (block_rows, LANES), 1)
    found = jnp.full((block_rows, LANES), -1, jnp.int32)
    for k in range(kept):
        found = jnp.where(slot == positions[:, k : k + 1], k, found)
    same_half = (found & 1) == (slot & 1)
    tile = found >> 1
    return jnp.where(found < 0, source_tiles, jnp.where(same_half, tile, tile + source_tiles + 1))


def place_and_multiply(tiles_ref, spread_ref, codes_smem, margin_ref, copies, parts, outs):
    block_rows, blocksize, lanes = tiles_ref.shape
    source_tiles = (lanes // LANES - 1) // 2
    turned_at = source_tiles + 1
    per_chunk = block_rows // CHUNKS
    width = margin_ref.shape[1]
    empty = slice(source_tiles * LANES, turned_at * LANES)
    tiles_ref[:, :, empty] = jnp.zeros((block_rows, blocksize, LANES), jnp.bfloat16)
    low_half = lax.broadcasted_iota(jnp.int32, (blocksize, LANES), 1) < blocksize
    per_part = width // LANES
    for c in range(CHUNKS):
        copies[c].wait()

        def place(i, carry):
            r = c * per_chunk + i
            first = pl.multiple_of(r * blocksize, blocksize)
            for t in range(source_tiles):
                at = (turned_at + t) * LANES
                tiles_ref[r, :, at : at + LANES] = pltpu.roll(
                    tiles_ref[r, :, t * LANES : (t + 1) * LANES], blocksize, 1
                )
            for n, part in enumerate(parts):
                for q in range(per_part):
                    at = 2 * (part * per_part + q)
                    left = pl.multiple_of(codes_smem[r, at] * LANES, LANES)
                    right = pl.multiple_of(codes_smem[r, at + 1] * LANES, LANES)
                    to = n * width + q * LANES
                    spread_ref[pl.ds(first, blocksize), to : to + LANES] = jnp.where(
                        low_half,
                        tiles_ref[r, :, pl.ds(left, LANES)],
                        tiles_ref[r, :, pl.ds(right, LANES)],
                    )
            return carry

        lax.fori_loop(0, per_chunk, place, 0)
    step = 256
    for n, out in enumerate(outs):
        for t in range(width // step):
            at = n * width + t * step
            out[:, t * step : (t + 1) * step] = jnp.dot(
                margin_ref[...], spread_ref[:, at : at + step], preferred_element_type=jnp.float32
            )


def first_kernel(
    total_blocks,
    base_ref,
    labels_hbm,
    cols_hbm,
    scores_hbm,
    weights_hbm,
    down_hbm,
    up_hbm,
    margin_hbm,
    codes_hbm,
    labels_ref,
    cols_ref,
    scores_ref,
    tiles_ref,
    spread_ref,
    codes_ref,
    codes_smem,
    margin_ref,
    parts_ref,
    small_sems,
    sems,
    part_sems,
):
    cols_copy = pltpu.make_async_copy(cols_hbm, cols_ref, small_sems.at[0])
    labels_copy = pltpu.make_async_copy(labels_hbm, labels_ref, small_sems.at[1])
    scores_copy = pltpu.make_async_copy(scores_hbm, scores_ref, small_sems.at[2])
    cols_copy.start()
    labels_copy.start()
    scores_copy.start()
    copies = start_weights(weights_hbm, tiles_ref, sems)
    block_rows, blocksize, packed = weights_hbm.shape
    classes, samples, width = scores_ref.shape
    source_tiles = packed // LANES
    turned_at = source_tiles + 1
    per_chunk = block_rows // CHUNKS
    depth = per_chunk * blocksize
    tiles_ref[:, :, packed : packed + LANES] = jnp.zeros((block_rows, blocksize, LANES), jnp.bfloat16)
    cols_copy.wait()
    codes_ref[...] = make_codes(cols_ref[...], base_ref[0], total_blocks, source_tiles)
    codes_copy = pltpu.make_async_copy(codes_ref, codes_smem, small_sems.at[3])
    codes_copy.start()
    codes_out = pltpu.make_async_copy(codes_ref, codes_hbm, small_sems.at[4])
    codes_out.start()
    labels_copy.wait()
    row = lax.broadcasted_iota(jnp.int32, (samples, width), 0)
    labels = jnp.zeros((samples, width), jnp.int32)
    for s in range(samples):
        labels = jnp.where(row == s, labels_ref[s], labels)
    scores_copy.wait()
    scores = [scores_ref[c].astype(jnp.float32) for c in range(classes)]
    top = scores[0]
    for c in range(1, classes):
        top = jnp.where(labels == c, scores[c], top)
    for j in range(classes - 1):
        rest = jnp.where(labels > j, scores[j], scores[j + 1])
        margin_ref[pl.ds(j * samples, samples), :] = (top - rest).astype(jnp.bfloat16)
    margin_out = pltpu.make_async_copy(margin_ref, margin_hbm, small_sems.at[5])
    margin_out.start()
    low_half = lax.broadcasted_iota(jnp.int32, (blocksize, LANES), 1) < blocksize
    per_part = width // LANES

    def turn(r):
        for t in range(source_tiles):
            at = (turned_at + t) * LANES
            tiles_ref[r, :, at : at + LANES] = pltpu.roll(
                tiles_ref[r, :, t * LANES : (t + 1) * LANES], blocksize, 1
            )

    def place(c, i):
        r = c * per_chunk + i
        for n, part in enumerate((0, 2)):
            for q in range(per_part):
                at = 2 * (part * per_part + q)
                left = pl.multiple_of(codes_smem[r, at] * LANES, LANES)
                right = pl.multiple_of(codes_smem[r, at + 1] * LANES, LANES)
                to = n * width + q * LANES
                spread_ref[c, i * blocksize : (i + 1) * blocksize, to : to + LANES] = jnp.where(
                    low_half,
                    tiles_ref[r, :, pl.ds(left, LANES)],
                    tiles_ref[r, :, pl.ds(right, LANES)],
                )

    outs = []

    def multiply(c):
        step = 256
        for t in range(2 * width // step):
            product = jnp.dot(
                margin_ref[:, c * depth : (c + 1) * depth],
                spread_ref[c, :, t * step : (t + 1) * step],
                preferred_element_type=jnp.float32,
            )
            at = slice(t * step, (t + 1) * step)
            parts_ref[:, at] = product if c == 0 else parts_ref[:, at] + product
            if c == CHUNKS - 1:
                to = down_hbm if t * step < width else up_hbm
                out = pltpu.make_async_copy(
                    parts_ref.at[:, pl.ds(t * step, step)],
                    to.at[:, pl.ds(t * step % width, step)],
                    part_sems.at[t],
                )
                out.start()
                outs.append(out)

    for c in range(CHUNKS):
        copies[c].wait()
        if c == 0:
            for i in range(per_chunk):
                turn(i)
            codes_copy.wait()
        else:
            multiply(c - 1)
            for i in range(per_chunk):
                turn(c * per_chunk + i)
        for i in range(per_chunk):
            place(c, i)
    multiply(CHUNKS - 1)
    for copy in outs + [codes_out, margin_out]:
        copy.wait()


def first(total_blocks, base, labels, cols, scores, weights):
    classes, samples, width = scores.shape
    rows = (classes - 1) * samples
    block_rows, blocksize, packed = weights.shape
    hbm = pl.BlockSpec(memory_space=pltpu.HBM)
    return pl.pallas_call(
        functools.partial(first_kernel, total_blocks),
        out_shape=(
            jax.ShapeDtypeStruct((rows, width), jnp.float32),
            jax.ShapeDtypeStruct((rows, width), jnp.float32),
            jax.ShapeDtypeStruct((rows, width), jnp.bfloat16),
            jax.ShapeDtypeStruct((block_rows, LANES), jnp.int32),
        ),
        in_specs=[pl.BlockSpec(memory_space=pltpu.SMEM), hbm, hbm, hbm, hbm],
        out_specs=(hbm, hbm, hbm, hbm),
        scratch_shapes=[
            pltpu.SMEM((samples,), jnp.int32),
            pltpu.VMEM(cols.shape, jnp.int32),
            pltpu.VMEM(scores.shape, jnp.bfloat16),
            pltpu.VMEM((block_rows, blocksize, 2 * packed + LANES), jnp.bfloat16),
            pltpu.VMEM((CHUNKS, block_rows * blocksize // CHUNKS, 2 * width), jnp.bfloat16),
            pltpu.VMEM((block_rows, LANES), jnp.int32),
            pltpu.SMEM((block_rows, LANES), jnp.int32),
            pltpu.VMEM((rows, width), jnp.bfloat16),
            pltpu.VMEM((rows, 2 * width), jnp.float32),
            pltpu.SemaphoreType.DMA((6,)),
            pltpu.SemaphoreType.DMA((CHUNKS,)),
            pltpu.SemaphoreType.DMA((2 * width // 256,)),
        ],
        compiler_params=pltpu.CompilerParams(vmem_limit_bytes=61 << 20),
        cost_estimate=pl.CostEstimate(
            flops=4 * rows * width * width, bytes_accessed=6 << 20, transcendentals=0
        ),
        name="first",
    )(base, labels, cols, scores, weights)


def second_kernel(
    codes_hbm, bias_ref, margin_ref, weights_hbm, centre_ref, bias_acc_ref, tiles_ref, spread_ref, codes_smem, small_sems, sems
):
    codes_copy = pltpu.make_async_copy(codes_hbm, codes_smem, small_sems.at[0])
    codes_copy.start()
    copies = start_weights(weights_hbm, tiles_ref, sems)
    width = margin_ref.shape[1]
    terms = margin_ref[...].astype(jnp.float32) * bias_ref[...]
    acc = terms[:, :LANES]
    for t in range(1, width // LANES):
        acc = acc + terms[:, t * LANES : (t + 1) * LANES]
    bias_acc_ref[...] = acc
    codes_copy.wait()
    place_and_multiply(tiles_ref, spread_ref, codes_smem, margin_ref, copies, (1,), (centre_ref,))


def second(codes, bias, margin, weights):
    rows, width = margin.shape
    block_rows, blocksize, packed = weights.shape
    hbm = pl.BlockSpec(memory_space=pltpu.HBM)
    vmem = pl.BlockSpec(memory_space=pltpu.VMEM)
    part = jax.ShapeDtypeStruct((rows, width), jnp.float32)
    return pl.pallas_call(
        second_kernel,
        out_shape=(part, jax.ShapeDtypeStruct((rows, LANES), jnp.float32)),
        in_specs=[vmem, vmem, vmem, hbm],
        out_specs=(vmem, vmem),
        scratch_shapes=[
            pltpu.VMEM((block_rows, blocksize, 2 * packed + LANES), jnp.bfloat16),
            pltpu.VMEM((block_rows * blocksize, width), jnp.bfloat16),
            pltpu.SMEM((block_rows, LANES), jnp.int32),
            pltpu.SemaphoreType.DMA((1,)),
            pltpu.SemaphoreType.DMA((CHUNKS,)),
        ],
        compiler_params=pltpu.CompilerParams(vmem_limit_bytes=30 << 20),
        cost_estimate=pl.CostEstimate(
            flops=2 * rows * width * width, bytes_accessed=6 << 20, transcendentals=0
        ),
        name="second",
    )(codes, bias, margin, weights)


def relax_kernel(
    flags_ref,
    mid_ref,
    rad_ref,
    slope_ref,
    bias_acc_ref,
    centre_ref,
    higher_ref,
    lower_ref,
    closing_ref,
    coef_ref,
    offs_ref,
    acc_ref,
):
    specs, samples, width = coef_ref.shape
    blocksize = width // flags_ref.shape[0]
    lower = mid_ref[...] - rad_ref[...]
    upper = mid_ref[...] + rad_ref[...]
    up_slope = (jnp.maximum(upper, 0.0) - jnp.maximum(lower, 0.0)) / (upper - lower)
    up_shift = jnp.maximum(lower, 0.0) - up_slope * lower
    block = lax.broadcasted_iota(jnp.int32, (1, width), 1) // blocksize
    flags = jnp.zeros((1, width), jnp.int32)
    for b in range(flags_ref.shape[0]):
        flags = jnp.where(block == b, flags_ref[b], flags)
    low_slope = jnp.where(flags == 1, slope_ref[...], up_slope)
    for j in range(specs):
        at = slice(j * samples, (j + 1) * samples)
        propagated = centre_ref[at] + higher_ref[at] + lower_ref[at] + closing_ref[at]
        negative = jnp.minimum(propagated, 0.0)
        coef_ref[j] = (low_slope * jnp.maximum(propagated, 0.0) + up_slope * negative).astype(jnp.bfloat16)
        terms = negative * up_shift
        acc = bias_acc_ref[at]
        for t in range(width // LANES):
            acc = acc + terms[:, t * LANES : (t + 1) * LANES]
        acc_ref[at] = acc
    sums = lax.dot_general(
        jnp.ones((8, LANES), jnp.float32),
        acc_ref[...],
        (((1,), (1,)), ((), ())),
        precision=lax.Precision.HIGHEST,
        preferred_element_type=jnp.float32,
    )
    for d in range(offs_ref.shape[0]):
        offs_ref[d] = sums[:1]


def relax(flags, mid, rad, slope, bias_acc, centre, higher, lower, closing, samples, devices):
    rows, width = centre.shape
    specs = rows // samples
    smem = pl.BlockSpec(memory_space=pltpu.SMEM)
    vmem = pl.BlockSpec(memory_space=pltpu.VMEM)
    return pl.pallas_call(
        relax_kernel,
        out_shape=(
            jax.ShapeDtypeStruct((specs, samples, width), jnp.bfloat16),
            jax.ShapeDtypeStruct((devices, 1, rows), jnp.float32),
        ),
        in_specs=[smem] + [vmem] * 8,
        out_specs=(vmem, vmem),
        scratch_shapes=[pltpu.VMEM((rows, LANES), jnp.float32)],
        compiler_params=pltpu.CompilerParams(vmem_limit_bytes=16 << 20),
        cost_estimate=pl.CostEstimate(
            flops=10 * rows * width, bytes_accessed=4 << 20, transcendentals=0
        ),
        name="relax",
    )(flags, mid, rad, slope, bias_acc, centre, higher, lower, closing)


def total_kernel(parts_ref, out_ref):
    specs, samples = out_ref.shape
    sums = parts_ref[0]
    for d in range(1, parts_ref.shape[0]):
        sums = sums + parts_ref[d]
    for j in range(specs):
        out_ref[j : j + 1, :] = sums[:, j * samples : (j + 1) * samples]


def local(
    class_scores,
    true_class,
    weight_blocks,
    col_blocks,
    layer_bias,
    bound_mid,
    bound_rad,
    lower_slope,
    unstable_blocks,
):
    samples, classes, width = class_scores.shape
    specs = classes - 1
    per_dev = col_blocks.shape[0]
    devices = lax.axis_size("neuron")
    position = lax.axis_index("neuron")
    base = ((position - 1) * per_dev).astype(jnp.int32).reshape(1)
    down, up, margin, codes = first(
        devices * per_dev,
        base,
        true_class,
        col_blocks,
        jnp.transpose(class_scores, (1, 0, 2)),
        weight_blocks,
    )
    starts = range(0, devices, RUN)
    ends = range(RUN - 1, devices, RUN)
    higher = send(down, [(i, i - 1) for i in range(devices) if i not in starts])
    lower = send(up, [(i, i + 1) for i in range(devices) if i not in ends])
    outer = jnp.where(position % RUN == 0, down, up)
    closing = send(
        outer,
        [(i, (i - 1) % devices) for i in starts] + [(i, (i + 1) % devices) for i in ends],
    )
    layer_bias, margin, weight_blocks = lax.optimization_barrier((layer_bias, margin, weight_blocks))
    bias = layer_bias.astype(jnp.float32).reshape(1, width)
    centre, bias_acc = second(codes, bias, margin, weight_blocks)
    coef, offs = relax(
        unstable_blocks,
        bound_mid.reshape(1, width),
        bound_rad.reshape(1, width),
        lower_slope.reshape(1, width),
        bias_acc,
        centre,
        higher,
        lower,
        closing,
        samples,
        devices,
    )
    gathered = lax.all_to_all(offs, "neuron", 0, 0)
    offsets = pl.pallas_call(
        total_kernel,
        out_shape=jax.ShapeDtypeStruct((specs, samples), jnp.float32),
        name="total",
    )(gathered)
    return jnp.transpose(coef, (1, 0, 2)), offsets.T


def solution(mesh):
    placed = (
        P("spec", None, "neuron"),
        P("spec"),
        P("neuron", None, None),
        P("neuron", None),
        P("neuron"),
        P("neuron"),
        P("neuron"),
        P("neuron"),
        P("neuron"),
    )
    return jax.shard_map(
        local,
        mesh=mesh,
        in_specs=placed,
        out_specs=(P("spec", None, "neuron"), P("spec", None)),
        check_vma=False,
    )
```

```python
import functools

import jax
import jax.numpy as jnp
from jax import lax
from jax.experimental import pallas as pl
from jax.experimental.pallas import tpu as pltpu
from jax.sharding import PartitionSpec as P


LANES = 128
CHUNKS = 2


RUN = 8


def send(value, pairs):
    return lax.ppermute(value, "neuron", pairs)


def start_weights(weights_hbm, tiles_ref, sems):
    block_rows, _, packed = weights_hbm.shape
    copies = [
        pltpu.make_async_copy(
            weights_hbm.at[r], tiles_ref.at[:, pl.ds(2 * packed * r, packed)], sems.at[r]
        )
        for r in range(block_rows)
    ]
    for copy in copies:
        copy.start()
    return copies


def make_codes(cols, base, total_blocks, source_tiles):
    block_rows, kept = cols.shape
    positions = (cols - base) & (total_blocks - 1)
    slot = lax.broadcasted_iota(jnp.int32, (block_rows, LANES), 1)
    own = lax.broadcasted_iota(jnp.int32, (block_rows, LANES), 0) * (2 * source_tiles)
    found = jnp.full((block_rows, LANES), -1, jnp.int32)
    for k in range(kept):
        found = jnp.where(slot == positions[:, k : k + 1], k, found)
    same_half = (found & 1) == (slot & 1)
    tile = own + (found >> 1)
    held = jnp.where(same_half, tile, tile + source_tiles)
    return jnp.where(found < 0, 2 * source_tiles * block_rows, held)


def turn(tiles_ref, r, packed, blocksize):
    for t in range(packed // LANES):
        at = 2 * packed * r + t * LANES
        tiles_ref[:, at + packed : at + packed + LANES] = pltpu.roll(
            tiles_ref[:, at : at + LANES], blocksize, 1
        )


def place(tiles_ref, spread_ref, codes_smem, c, i, r, parts, width):
    blocksize = tiles_ref.shape[0]
    low_half = lax.broadcasted_iota(jnp.int32, (blocksize, LANES), 1) < blocksize
    per_part = width // LANES
    for n, part in enumerate(parts):
        for q in range(per_part):
            at = 2 * (part * per_part + q)
            left = pl.multiple_of(codes_smem[r, at] * LANES, LANES)
            right = pl.multiple_of(codes_smem[r, at + 1] * LANES, LANES)
            to = n * width + q * LANES
            spread_ref[c, i * blocksize : (i + 1) * blocksize, to : to + LANES] = jnp.where(
                low_half, tiles_ref[:, pl.ds(left, LANES)], tiles_ref[:, pl.ds(right, LANES)]
            )


def multiply(margin_ref, spread_ref, c, outs):
    depth, total = spread_ref.shape[1:]
    width = total // len(outs)
    step = 256
    for t in range(total // step):
        product = jnp.dot(
            margin_ref[:, c * depth : (c + 1) * depth],
            spread_ref[c, :, t * step : (t + 1) * step],
            preferred_element_type=jnp.float32,
        )
        out = outs[t * step // width]
        at = slice(t * step % width, t * step % width + step)
        out[:, at] = product if c == 0 else out[:, at] + product


def place_and_multiply(tiles_ref, spread_ref, codes_smem, codes_copy, margin_ref, copies, parts, outs):
    blocksize = tiles_ref.shape[0]
    block_rows = len(copies)
    packed = (tiles_ref.shape[1] - LANES) // (2 * block_rows)
    per_chunk = block_rows // CHUNKS
    width = margin_ref.shape[1]
    tiles_ref[:, tiles_ref.shape[1] - LANES :] = jnp.zeros((blocksize, LANES), jnp.bfloat16)
    for c in range(CHUNKS):
        rows = range(c * per_chunk, (c + 1) * per_chunk)
        for r in rows:
            copies[r].wait()
        if c > 0:
            multiply(margin_ref, spread_ref, c - 1, outs)
        for r in rows:
            turn(tiles_ref, r, packed, blocksize)
        if c == 0:
            codes_copy.wait()
        for i, r in enumerate(rows):
            place(tiles_ref, spread_ref, codes_smem, c, i, r, parts, width)
    multiply(margin_ref, spread_ref, CHUNKS - 1, outs)


def tile_scratch(weights, parts, width):
    block_rows, blocksize, packed = weights.shape
    return [
        pltpu.VMEM((blocksize, block_rows * 2 * packed + LANES), jnp.bfloat16),
        pltpu.VMEM((CHUNKS, block_rows * blocksize // CHUNKS, parts * width), jnp.bfloat16),
    ]


def first_kernel(
    total_blocks,
    base_ref,
    labels_hbm,
    cols_hbm,
    scores_hbm,
    weights_hbm,
    down_ref,
    up_ref,
    margin_hbm,
    codes_ref,
    labels_ref,
    cols_ref,
    scores_ref,
    margin_ref,
    tiles_ref,
    spread_ref,
    codes_smem,
    small_sems,
    sems,
):
    cols_copy = pltpu.make_async_copy(cols_hbm, cols_ref, small_sems.at[0])
    labels_copy = pltpu.make_async_copy(labels_hbm, labels_ref, small_sems.at[1])
    scores_copy = pltpu.make_async_copy(scores_hbm, scores_ref, small_sems.at[2])
    cols_copy.start()
    labels_copy.start()
    scores_copy.start()
    copies = start_weights(weights_hbm, tiles_ref, sems)
    classes, samples, width = scores_ref.shape
    cols_copy.wait()
    codes_ref[...] = make_codes(
        cols_ref[...], base_ref[0], total_blocks, weights_hbm.shape[2] // LANES
    )
    codes_copy = pltpu.make_async_copy(codes_ref, codes_smem, small_sems.at[3])
    codes_copy.start()
    labels_copy.wait()
    row = lax.broadcasted_iota(jnp.int32, (samples, width), 0)
    labels = jnp.zeros((samples, width), jnp.int32)
    for s in range(samples):
        labels = jnp.where(row == s, labels_ref[s], labels)
    scores_copy.wait()
    scores = [scores_ref[c].astype(jnp.float32) for c in range(classes)]
    top = scores[0]
    for c in range(1, classes):
        top = jnp.where(labels == c, scores[c], top)
    for j in range(classes - 1):
        rest = jnp.where(labels > j, scores[j], scores[j + 1])
        margin_ref[pl.ds(j * samples, samples), :] = (top - rest).astype(jnp.bfloat16)
    margin_copy = pltpu.make_async_copy(margin_ref, margin_hbm, small_sems.at[4])
    margin_copy.start()
    place_and_multiply(
        tiles_ref, spread_ref, codes_smem, codes_copy, margin_ref, copies, (0, 2), (down_ref, up_ref)
    )
    margin_copy.wait()


def first(total_blocks, base, labels, cols, scores, weights):
    classes, samples, width = scores.shape
    rows = (classes - 1) * samples
    block_rows = weights.shape[0]
    hbm = pl.BlockSpec(memory_space=pltpu.HBM)
    vmem = pl.BlockSpec(memory_space=pltpu.VMEM)
    return pl.pallas_call(
        functools.partial(first_kernel, total_blocks),
        out_shape=(
            pltpu.VMEM((rows, width), jnp.float32),
            pltpu.VMEM((rows, width), jnp.float32),
            jax.ShapeDtypeStruct((rows, width), jnp.bfloat16),
            pltpu.VMEM((block_rows, LANES), jnp.int32),
        ),
        in_specs=[pl.BlockSpec(memory_space=pltpu.SMEM), hbm, hbm, hbm, hbm],
        out_specs=(vmem, vmem, hbm, vmem),
        scratch_shapes=[
            pltpu.SMEM((samples,), jnp.int32),
            pltpu.VMEM(cols.shape, jnp.int32),
            pltpu.VMEM(scores.shape, jnp.bfloat16),
            pltpu.VMEM((rows, width), jnp.bfloat16),
            *tile_scratch(weights, 2, width),
            pltpu.SMEM((block_rows, LANES), jnp.int32),
            pltpu.SemaphoreType.DMA((5,)),
            pltpu.SemaphoreType.DMA((block_rows,)),
        ],
        compiler_params=pltpu.CompilerParams(vmem_limit_bytes=60 << 20),
        cost_estimate=pl.CostEstimate(
            flops=4 * rows * width * width, bytes_accessed=6 << 20, transcendentals=0
        ),
        name="first",
    )(base, labels, cols, scores, weights)


def second_kernel(
    flags_ref,
    codes_vmem,
    bias_ref,
    mid_ref,
    rad_ref,
    slope_ref,
    margin_hbm,
    weights_hbm,
    centre_ref,
    bias_acc_ref,
    slopes_ref,
    margin_ref,
    tiles_ref,
    spread_ref,
    codes_smem,
    small_sems,
    sems,
):
    codes_copy = pltpu.make_async_copy(codes_vmem, codes_smem, small_sems.at[0])
    codes_copy.start()
    margin_copy = pltpu.make_async_copy(margin_hbm, margin_ref, small_sems.at[1])
    margin_copy.start()
    copies = start_weights(weights_hbm, tiles_ref, sems)
    width = margin_ref.shape[1]
    margin_copy.wait()
    terms = margin_ref[...].astype(jnp.float32) * bias_ref[...]
    acc = terms[:, :LANES]
    for t in range(1, width // LANES):
        acc = acc + terms[:, t * LANES : (t + 1) * LANES]
    bias_acc_ref[...] = acc
    lower = mid_ref[...] - rad_ref[...]
    upper = mid_ref[...] + rad_ref[...]
    up_slope = (jnp.maximum(upper, 0.0) - jnp.maximum(lower, 0.0)) / (upper - lower)
    blocks = flags_ref.shape[0]
    block = lax.broadcasted_iota(jnp.int32, (1, width), 1) // (width // blocks)
    flags = jnp.zeros((1, width), jnp.int32)
    for b in range(blocks):
        flags = jnp.where(block == b, flags_ref[b], flags)
    slopes_ref[0:1] = jnp.where(flags == 1, slope_ref[...], up_slope)
    slopes_ref[1:2] = up_slope
    slopes_ref[2:3] = jnp.maximum(lower, 0.0) - up_slope * lower
    place_and_multiply(
        tiles_ref, spread_ref, codes_smem, codes_copy, margin_ref, copies, (1,), (centre_ref,)
    )


def second(flags, codes, bias, mid, rad, slope, margin, weights):
    rows, width = margin.shape
    block_rows = weights.shape[0]
    vmem = pl.BlockSpec(memory_space=pltpu.VMEM)
    return pl.pallas_call(
        second_kernel,
        out_shape=(
            pltpu.VMEM((rows, width), jnp.float32),
            pltpu.VMEM((rows, LANES), jnp.float32),
            pltpu.VMEM((3, width), jnp.float32),
        ),
        in_specs=[pl.BlockSpec(memory_space=pltpu.SMEM)]
        + [vmem] * 5
        + [pl.BlockSpec(memory_space=pltpu.HBM)] * 2,
        out_specs=(vmem, vmem, vmem),
        scratch_shapes=[
            pltpu.VMEM((rows, width), jnp.bfloat16),
            *tile_scratch(weights, 1, width),
            pltpu.SMEM((block_rows, LANES), jnp.int32),
            pltpu.SemaphoreType.DMA((2,)),
            pltpu.SemaphoreType.DMA((block_rows,)),
        ],
        compiler_params=pltpu.CompilerParams(vmem_limit_bytes=30 << 20),
        cost_estimate=pl.CostEstimate(
            flops=2 * rows * width * width, bytes_accessed=6 << 20, transcendentals=0
        ),
        name="second",
    )(flags, codes, bias, mid, rad, slope, margin, weights)


def sums_kernel(slopes_ref, bias_acc_ref, centre_ref, higher_ref, lower_ref, closing_ref, offs_ref, acc_ref):
    rows, width = centre_ref.shape
    up_shift = slopes_ref[2:3]
    part = 24
    for first_row in range(0, rows, part):
        at = slice(first_row, first_row + part)
        propagated = centre_ref[at] + higher_ref[at] + lower_ref[at] + closing_ref[at]
        terms = jnp.minimum(propagated, 0.0) * up_shift
        acc = bias_acc_ref[at]
        for t in range(width // LANES):
            acc = acc + terms[:, t * LANES : (t + 1) * LANES]
        acc_ref[at] = acc
    sums = lax.dot_general(
        jnp.ones((8, LANES), jnp.float32),
        acc_ref[...],
        (((1,), (1,)), ((), ())),
        precision=lax.Precision.HIGHEST,
        preferred_element_type=jnp.float32,
    )
    for d in range(offs_ref.shape[0]):
        offs_ref[d] = sums[:1]


def sums(devices, slopes, bias_acc, centre, higher, lower, closing):
    rows, _ = centre.shape
    vmem = pl.BlockSpec(memory_space=pltpu.VMEM)
    return pl.pallas_call(
        sums_kernel,
        out_shape=pltpu.VMEM((devices, 1, rows), jnp.float32),
        in_specs=[vmem] * 6,
        out_specs=vmem,
        scratch_shapes=[pltpu.VMEM((rows, LANES), jnp.float32)],
        compiler_params=pltpu.CompilerParams(vmem_limit_bytes=16 << 20),
        name="sums",
    )(slopes, bias_acc, centre, higher, lower, closing)


def last_kernel(
    slopes_ref,
    centre_ref,
    higher_ref,
    lower_ref,
    closing_ref,
    gathered_ref,
    coef_hbm,
    out_ref,
    coef_ref,
    coef_sems,
):
    specs, samples, _ = coef_ref.shape
    low_slope = slopes_ref[0:1]
    up_slope = slopes_ref[1:2]
    copies = []
    for j in range(specs):
        at = slice(j * samples, (j + 1) * samples)
        propagated = centre_ref[at] + higher_ref[at] + lower_ref[at] + closing_ref[at]
        positive = jnp.maximum(propagated, 0.0)
        negative = jnp.minimum(propagated, 0.0)
        coef_ref[j] = (low_slope * positive + up_slope * negative).astype(jnp.bfloat16)
        copies.append(pltpu.make_async_copy(coef_ref.at[j], coef_hbm.at[j], coef_sems.at[j]))
        copies[-1].start()
    total = gathered_ref[0]
    for d in range(1, gathered_ref.shape[0]):
        total = total + gathered_ref[d]
    for j in range(specs):
        out_ref[j : j + 1, :] = total[:, j * samples : (j + 1) * samples]
    for copy in copies:
        copy.wait()


def last(samples, slopes, centre, higher, lower, closing, gathered):
    rows, width = centre.shape
    specs = rows // samples
    vmem = pl.BlockSpec(memory_space=pltpu.VMEM)
    hbm = pl.BlockSpec(memory_space=pltpu.HBM)
    return pl.pallas_call(
        last_kernel,
        out_shape=(
            jax.ShapeDtypeStruct((specs, samples, width), jnp.bfloat16),
            jax.ShapeDtypeStruct((specs, samples), jnp.float32),
        ),
        in_specs=[vmem] * 6,
        out_specs=(hbm, vmem),
        scratch_shapes=[
            pltpu.VMEM((specs, samples, width), jnp.bfloat16),
            pltpu.SemaphoreType.DMA((specs,)),
        ],
        compiler_params=pltpu.CompilerParams(vmem_limit_bytes=16 << 20),
        name="last",
    )(slopes, centre, higher, lower, closing, gathered)


def local(
    class_scores,
    true_class,
    weight_blocks,
    col_blocks,
    layer_bias,
    bound_mid,
    bound_rad,
    lower_slope,
    unstable_blocks,
):
    samples, _, width = class_scores.shape
    per_dev = col_blocks.shape[0]
    devices = lax.axis_size("neuron")
    position = lax.axis_index("neuron")
    base = ((position - 1) * per_dev).astype(jnp.int32).reshape(1)
    down, up, margin, codes = first(
        devices * per_dev,
        base,
        true_class,
        col_blocks,
        jnp.transpose(class_scores, (1, 0, 2)),
        weight_blocks,
    )
    starts = range(0, devices, RUN)
    ends = range(RUN - 1, devices, RUN)
    higher = send(down, [(i, i - 1) for i in range(devices) if i not in starts])
    lower = send(up, [(i, i + 1) for i in range(devices) if i not in ends])
    outer = jnp.where(position % RUN == 0, down, up)
    closing = send(
        outer,
        [(i, (i - 1) % devices) for i in starts] + [(i, (i + 1) % devices) for i in ends],
    )
    bias = layer_bias.astype(jnp.float32).reshape(1, width)
    centre, bias_acc, slopes = second(
        unstable_blocks,
        codes,
        bias,
        bound_mid.reshape(1, width),
        bound_rad.reshape(1, width),
        lower_slope.reshape(1, width),
        margin,
        weight_blocks,
    )
    offs = sums(devices, slopes, bias_acc, centre, higher, lower, closing)
    gathered = lax.all_to_all(offs, "neuron", 0, 0)
    coef, offsets = last(samples, slopes, centre, higher, lower, closing, gathered)
    return jnp.transpose(coef, (1, 0, 2)), offsets.T


def solution(mesh):
    placed = (
        P("spec", None, "neuron"),
        P("spec"),
        P("neuron", None, None),
        P("neuron", None),
        P("neuron"),
        P("neuron"),
        P("neuron"),
        P("neuron"),
        P("neuron"),
    )
    return jax.shard_map(
        local,
        mesh=mesh,
        in_specs=placed,
        out_specs=(P("spec", None, "neuron"), P("spec", None)),
        check_vma=False,
    )
```

```python
import functools

import jax
import jax.numpy as jnp
from jax import lax
from jax.experimental import pallas as pl
from jax.experimental.pallas import tpu as pltpu
from jax.sharding import PartitionSpec as P


LANES = 128
CHUNKS = 2


RUN = 8


def send(value, pairs):
    return lax.ppermute(value, "neuron", pairs)


def start_weights(weights_hbm, tiles_ref, sems):
    block_rows, _, packed = weights_hbm.shape
    copies = [
        pltpu.make_async_copy(
            weights_hbm.at[r], tiles_ref.at[:, pl.ds(2 * packed * r, packed)], sems.at[r]
        )
        for r in range(block_rows)
    ]
    for copy in copies:
        copy.start()
    return copies


def make_codes(cols, base, total_blocks, source_tiles):
    block_rows, kept = cols.shape
    positions = (cols - base) & (total_blocks - 1)
    slot = lax.broadcasted_iota(jnp.int32, (block_rows, LANES), 1)
    own = lax.broadcasted_iota(jnp.int32, (block_rows, LANES), 0) * (2 * source_tiles)
    found = jnp.full((block_rows, LANES), -1, jnp.int32)
    for k in range(kept):
        found = jnp.where(slot == positions[:, k : k + 1], k, found)
    same_half = (found & 1) == (slot & 1)
    tile = own + (found >> 1)
    held = jnp.where(same_half, tile, tile + source_tiles)
    return jnp.where(found < 0, 2 * source_tiles * block_rows, held)


def turn(tiles_ref, r, packed, blocksize):
    for t in range(packed // LANES):
        at = 2 * packed * r + t * LANES
        tiles_ref[:, at + packed : at + packed + LANES] = pltpu.roll(
            tiles_ref[:, at : at + LANES], blocksize, 1
        )


def place(tiles_ref, spread_ref, codes_smem, c, i, r, parts, width):
    blocksize = tiles_ref.shape[0]
    low_half = lax.broadcasted_iota(jnp.int32, (blocksize, LANES), 1) < blocksize
    per_part = width // LANES
    for n, part in enumerate(parts):
        for q in range(per_part):
            at = 2 * (part * per_part + q)
            left = pl.multiple_of(codes_smem[r, at] * LANES, LANES)
            right = pl.multiple_of(codes_smem[r, at + 1] * LANES, LANES)
            to = n * width + q * LANES
            spread_ref[c, i * blocksize : (i + 1) * blocksize, to : to + LANES] = jnp.where(
                low_half, tiles_ref[:, pl.ds(left, LANES)], tiles_ref[:, pl.ds(right, LANES)]
            )


def multiply(margin_ref, spread_ref, c, outs):
    depth, total = spread_ref.shape[1:]
    width = total // len(outs)
    step = 256
    for t in range(total // step):
        product = jnp.dot(
            margin_ref[:, c * depth : (c + 1) * depth],
            spread_ref[c, :, t * step : (t + 1) * step],
            preferred_element_type=jnp.float32,
        )
        out = outs[t * step // width]
        at = slice(t * step % width, t * step % width + step)
        out[:, at] = product if c == 0 else out[:, at] + product


def place_and_multiply(
    tiles_ref, spread_ref, codes_smem, codes_copy, margin_ref, copies, parts, outs, prepare
):
    blocksize = tiles_ref.shape[0]
    block_rows = len(copies)
    packed = (tiles_ref.shape[1] - LANES) // (2 * block_rows)
    per_chunk = block_rows // CHUNKS
    width = margin_ref.shape[1]
    tiles_ref[:, tiles_ref.shape[1] - LANES :] = jnp.zeros((blocksize, LANES), jnp.bfloat16)
    for c in range(CHUNKS):
        rows = range(c * per_chunk, (c + 1) * per_chunk)
        for r in rows:
            copies[r].wait()
        for r in rows:
            turn(tiles_ref, r, packed, blocksize)
        if c == 0:
            prepare()
            codes_copy.wait()
        for i, r in enumerate(rows):
            place(tiles_ref, spread_ref, codes_smem, c, i, r, parts, width)
        if c > 0:
            multiply(margin_ref, spread_ref, c - 1, outs)
    multiply(margin_ref, spread_ref, CHUNKS - 1, outs)


def tile_scratch(weights, parts, width):
    block_rows, blocksize, packed = weights.shape
    return [
        pltpu.VMEM((blocksize, block_rows * 2 * packed + LANES), jnp.bfloat16),
        pltpu.VMEM((CHUNKS, block_rows * blocksize // CHUNKS, parts * width), jnp.bfloat16),
    ]


def first_kernel(
    total_blocks,
    base_ref,
    labels_hbm,
    cols_hbm,
    scores_hbm,
    weights_hbm,
    down_ref,
    up_ref,
    margin_hbm,
    codes_ref,
    labels_ref,
    cols_ref,
    scores_ref,
    margin_ref,
    tiles_ref,
    spread_ref,
    codes_smem,
    small_sems,
    sems,
):
    cols_copy = pltpu.make_async_copy(cols_hbm, cols_ref, small_sems.at[0])
    labels_copy = pltpu.make_async_copy(labels_hbm, labels_ref, small_sems.at[1])
    scores_copy = pltpu.make_async_copy(scores_hbm, scores_ref, small_sems.at[2])
    cols_copy.start()
    labels_copy.start()
    scores_copy.start()
    copies = start_weights(weights_hbm, tiles_ref, sems)
    classes, samples, width = scores_ref.shape
    cols_copy.wait()
    codes_ref[...] = make_codes(
        cols_ref[...], base_ref[0], total_blocks, weights_hbm.shape[2] // LANES
    )
    codes_copy = pltpu.make_async_copy(codes_ref, codes_smem, small_sems.at[3])
    codes_copy.start()
    margin_copy = pltpu.make_async_copy(margin_ref, margin_hbm, small_sems.at[4])

    def prepare():
        labels_copy.wait()
        row = lax.broadcasted_iota(jnp.int32, (samples, width), 0)
        labels = jnp.zeros((samples, width), jnp.int32)
        for s in range(samples):
            labels = jnp.where(row == s, labels_ref[s], labels)
        scores_copy.wait()
        scores = [scores_ref[c].astype(jnp.float32) for c in range(classes)]
        top = scores[0]
        for c in range(1, classes):
            top = jnp.where(labels == c, scores[c], top)
        for j in range(classes - 1):
            rest = jnp.where(labels > j, scores[j], scores[j + 1])
            margin_ref[pl.ds(j * samples, samples), :] = (top - rest).astype(jnp.bfloat16)
        margin_copy.start()

    place_and_multiply(
        tiles_ref, spread_ref, codes_smem, codes_copy, margin_ref, copies, (0, 2), (down_ref, up_ref), prepare
    )
    margin_copy.wait()


def first(total_blocks, base, labels, cols, scores, weights):
    classes, samples, width = scores.shape
    rows = (classes - 1) * samples
    block_rows = weights.shape[0]
    hbm = pl.BlockSpec(memory_space=pltpu.HBM)
    vmem = pl.BlockSpec(memory_space=pltpu.VMEM)
    return pl.pallas_call(
        functools.partial(first_kernel, total_blocks),
        out_shape=(
            pltpu.VMEM((rows, width), jnp.float32),
            pltpu.VMEM((rows, width), jnp.float32),
            jax.ShapeDtypeStruct((rows, width), jnp.bfloat16),
            pltpu.VMEM((block_rows, LANES), jnp.int32),
        ),
        in_specs=[pl.BlockSpec(memory_space=pltpu.SMEM), hbm, hbm, hbm, hbm],
        out_specs=(vmem, vmem, hbm, vmem),
        scratch_shapes=[
            pltpu.SMEM((samples,), jnp.int32),
            pltpu.VMEM(cols.shape, jnp.int32),
            pltpu.VMEM(scores.shape, jnp.bfloat16),
            pltpu.VMEM((rows, width), jnp.bfloat16),
            *tile_scratch(weights, 2, width),
            pltpu.SMEM((block_rows, LANES), jnp.int32),
            pltpu.SemaphoreType.DMA((5,)),
            pltpu.SemaphoreType.DMA((block_rows,)),
        ],
        compiler_params=pltpu.CompilerParams(vmem_limit_bytes=60 << 20),
        cost_estimate=pl.CostEstimate(
            flops=4 * rows * width * width, bytes_accessed=6 << 20, transcendentals=0
        ),
        name="first",
    )(base, labels, cols, scores, weights)


def second_kernel(
    flags_ref,
    codes_vmem,
    bias_ref,
    mid_ref,
    rad_ref,
    slope_ref,
    margin_hbm,
    weights_hbm,
    centre_ref,
    bias_acc_ref,
    slopes_ref,
    margin_ref,
    tiles_ref,
    spread_ref,
    codes_smem,
    small_sems,
    sems,
):
    codes_copy = pltpu.make_async_copy(codes_vmem, codes_smem, small_sems.at[0])
    codes_copy.start()
    margin_copy = pltpu.make_async_copy(margin_hbm, margin_ref, small_sems.at[1])
    margin_copy.start()
    copies = start_weights(weights_hbm, tiles_ref, sems)
    width = margin_ref.shape[1]
    margin_copy.wait()
    terms = margin_ref[...].astype(jnp.float32) * bias_ref[...]
    acc = terms[:, :LANES]
    for t in range(1, width // LANES):
        acc = acc + terms[:, t * LANES : (t + 1) * LANES]
    bias_acc_ref[...] = acc
    lower = mid_ref[...] - rad_ref[...]
    upper = mid_ref[...] + rad_ref[...]
    up_slope = (jnp.maximum(upper, 0.0) - jnp.maximum(lower, 0.0)) / (upper - lower)
    blocks = flags_ref.shape[0]
    block = lax.broadcasted_iota(jnp.int32, (1, width), 1) // (width // blocks)
    flags = jnp.zeros((1, width), jnp.int32)
    for b in range(blocks):
        flags = jnp.where(block == b, flags_ref[b], flags)
    slopes_ref[0:1] = jnp.where(flags == 1, slope_ref[...], up_slope)
    slopes_ref[1:2] = up_slope
    slopes_ref[2:3] = jnp.maximum(lower, 0.0) - up_slope * lower
    place_and_multiply(
        tiles_ref, spread_ref, codes_smem, codes_copy, margin_ref, copies, (1,), (centre_ref,), lambda: None
    )


def second(flags, codes, bias, mid, rad, slope, margin, weights):
    rows, width = margin.shape
    block_rows = weights.shape[0]
    vmem = pl.BlockSpec(memory_space=pltpu.VMEM)
    return pl.pallas_call(
        second_kernel,
        out_shape=(
            pltpu.VMEM((rows, width), jnp.float32),
            pltpu.VMEM((rows, LANES), jnp.float32),
            pltpu.VMEM((3, width), jnp.float32),
        ),
        in_specs=[pl.BlockSpec(memory_space=pltpu.SMEM)]
        + [vmem] * 5
        + [pl.BlockSpec(memory_space=pltpu.HBM)] * 2,
        out_specs=(vmem, vmem, vmem),
        scratch_shapes=[
            pltpu.VMEM((rows, width), jnp.bfloat16),
            *tile_scratch(weights, 1, width),
            pltpu.SMEM((block_rows, LANES), jnp.int32),
            pltpu.SemaphoreType.DMA((2,)),
            pltpu.SemaphoreType.DMA((block_rows,)),
        ],
        compiler_params=pltpu.CompilerParams(vmem_limit_bytes=30 << 20),
        cost_estimate=pl.CostEstimate(
            flops=2 * rows * width * width, bytes_accessed=6 << 20, transcendentals=0
        ),
        name="second",
    )(flags, codes, bias, mid, rad, slope, margin, weights)


def sums_kernel(slopes_ref, bias_acc_ref, centre_ref, higher_ref, lower_ref, closing_ref, offs_ref, acc_ref):
    rows, width = centre_ref.shape
    up_shift = slopes_ref[2:3]
    part = 24
    for first_row in range(0, rows, part):
        at = slice(first_row, first_row + part)
        propagated = centre_ref[at] + higher_ref[at] + lower_ref[at] + closing_ref[at]
        terms = jnp.minimum(propagated, 0.0) * up_shift
        acc = bias_acc_ref[at]
        for t in range(width // LANES):
            acc = acc + terms[:, t * LANES : (t + 1) * LANES]
        acc_ref[at] = acc
    sums = lax.dot_general(
        jnp.ones((8, LANES), jnp.float32),
        acc_ref[...],
        (((1,), (1,)), ((), ())),
        precision=lax.Precision.HIGHEST,
        preferred_element_type=jnp.float32,
    )
    for d in range(offs_ref.shape[0]):
        offs_ref[d] = sums[:1]


def sums(devices, slopes, bias_acc, centre, higher, lower, closing):
    rows, _ = centre.shape
    vmem = pl.BlockSpec(memory_space=pltpu.VMEM)
    return pl.pallas_call(
        sums_kernel,
        out_shape=pltpu.VMEM((devices, 1, rows), jnp.float32),
        in_specs=[vmem] * 6,
        out_specs=vmem,
        scratch_shapes=[pltpu.VMEM((rows, LANES), jnp.float32)],
        compiler_params=pltpu.CompilerParams(vmem_limit_bytes=16 << 20),
        name="sums",
    )(slopes, bias_acc, centre, higher, lower, closing)


def last_kernel(
    slopes_ref,
    centre_ref,
    higher_ref,
    lower_ref,
    closing_ref,
    gathered_ref,
    coef_hbm,
    out_hbm,
    coef_ref,
    out_ref,
    coef_sems,
    out_sem,
):
    specs, samples, _ = coef_ref.shape
    total = gathered_ref[0]
    for d in range(1, gathered_ref.shape[0]):
        total = total + gathered_ref[d]
    for j in range(specs):
        out_ref[j : j + 1, :] = total[:, j * samples : (j + 1) * samples]
    copies = [pltpu.make_async_copy(out_ref, out_hbm, out_sem)]
    copies[0].start()
    low_slope = slopes_ref[0:1]
    up_slope = slopes_ref[1:2]
    for j in range(specs):
        at = slice(j * samples, (j + 1) * samples)
        propagated = centre_ref[at] + higher_ref[at] + lower_ref[at] + closing_ref[at]
        positive = jnp.maximum(propagated, 0.0)
        negative = jnp.minimum(propagated, 0.0)
        coef_ref[j] = (low_slope * positive + up_slope * negative).astype(jnp.bfloat16)
        copies.append(pltpu.make_async_copy(coef_ref.at[j], coef_hbm.at[j], coef_sems.at[j]))
        copies[-1].start()
    for copy in copies:
        copy.wait()


def last(samples, slopes, centre, higher, lower, closing, gathered):
    rows, width = centre.shape
    specs = rows // samples
    vmem = pl.BlockSpec(memory_space=pltpu.VMEM)
    hbm = pl.BlockSpec(memory_space=pltpu.HBM)
    return pl.pallas_call(
        last_kernel,
        out_shape=(
            jax.ShapeDtypeStruct((specs, samples, width), jnp.bfloat16),
            jax.ShapeDtypeStruct((specs, samples), jnp.float32),
        ),
        in_specs=[vmem] * 6,
        out_specs=(hbm, hbm),
        scratch_shapes=[
            pltpu.VMEM((specs, samples, width), jnp.bfloat16),
            pltpu.VMEM((specs, samples), jnp.float32),
            pltpu.SemaphoreType.DMA((specs,)),
            pltpu.SemaphoreType.DMA,
        ],
        compiler_params=pltpu.CompilerParams(vmem_limit_bytes=16 << 20),
        name="last",
    )(slopes, centre, higher, lower, closing, gathered)


def local(
    class_scores,
    true_class,
    weight_blocks,
    col_blocks,
    layer_bias,
    bound_mid,
    bound_rad,
    lower_slope,
    unstable_blocks,
):
    samples, _, width = class_scores.shape
    per_dev = col_blocks.shape[0]
    devices = lax.axis_size("neuron")
    position = lax.axis_index("neuron")
    base = ((position - 1) * per_dev).astype(jnp.int32).reshape(1)
    down, up, margin, codes = first(
        devices * per_dev,
        base,
        true_class,
        col_blocks,
        jnp.transpose(class_scores, (1, 0, 2)),
        weight_blocks,
    )
    starts = range(0, devices, RUN)
    ends = range(RUN - 1, devices, RUN)
    higher = send(down, [(i, i - 1) for i in range(devices) if i not in starts])
    lower = send(up, [(i, i + 1) for i in range(devices) if i not in ends])
    outer = jnp.where(position % RUN == 0, down, up)
    closing = send(
        outer,
        [(i, (i - 1) % devices) for i in starts] + [(i, (i + 1) % devices) for i in ends],
    )
    bias = layer_bias.astype(jnp.float32).reshape(1, width)
    centre, bias_acc, slopes = second(
        unstable_blocks,
        codes,
        bias,
        bound_mid.reshape(1, width),
        bound_rad.reshape(1, width),
        lower_slope.reshape(1, width),
        margin,
        weight_blocks,
    )
    offs = sums(devices, slopes, bias_acc, centre, higher, lower, closing)
    gathered = lax.all_to_all(offs, "neuron", 0, 0)
    coef, offsets = last(samples, slopes, centre, higher, lower, closing, gathered)
    return jnp.transpose(coef, (1, 0, 2)), offsets.T


def solution(mesh):
    placed = (
        P("spec", None, "neuron"),
        P("spec"),
        P("neuron", None, None),
        P("neuron", None),
        P("neuron"),
        P("neuron"),
        P("neuron"),
        P("neuron"),
        P("neuron"),
    )
    return jax.shard_map(
        local,
        mesh=mesh,
        in_specs=placed,
        out_specs=(P("spec", None, "neuron"), P("spec", None)),
        check_vma=False,
    )
```

```python
import functools

import jax
import jax.numpy as jnp
from jax import lax
from jax.experimental import pallas as pl
from jax.experimental.pallas import tpu as pltpu
from jax.sharding import PartitionSpec as P


LANES = 128
CHUNKS = 2


RUN = 8


def send(value, pairs):
    return lax.ppermute(value, "neuron", pairs)


def start_weights(weights_hbm, tiles_ref, sems):
    block_rows, _, packed = weights_hbm.shape
    copies = [
        pltpu.make_async_copy(
            weights_hbm.at[r], tiles_ref.at[:, pl.ds(2 * packed * r, packed)], sems.at[r]
        )
        for r in range(block_rows)
    ]
    for copy in copies:
        copy.start()
    return copies


def make_codes(cols, base, total_blocks, source_tiles):
    block_rows, kept = cols.shape
    positions = (cols - base) & (total_blocks - 1)
    slot = lax.broadcasted_iota(jnp.int32, (block_rows, LANES), 1)
    own = lax.broadcasted_iota(jnp.int32, (block_rows, LANES), 0) * (2 * source_tiles)
    found = jnp.full((block_rows, LANES), -1, jnp.int32)
    for k in range(kept):
        found = jnp.where(slot == positions[:, k : k + 1], k, found)
    same_half = (found & 1) == (slot & 1)
    tile = own + (found >> 1)
    held = jnp.where(same_half, tile, tile + source_tiles)
    return jnp.where(found < 0, 2 * source_tiles * block_rows, held)


def turn(tiles_ref, r, packed, blocksize):
    for t in range(packed // LANES):
        at = 2 * packed * r + t * LANES
        tiles_ref[:, at + packed : at + packed + LANES] = pltpu.roll(
            tiles_ref[:, at : at + LANES], blocksize, 1
        )


def place(tiles_ref, spread_ref, codes_smem, c, i, r, parts, width):
    blocksize = tiles_ref.shape[0]
    low_half = lax.broadcasted_iota(jnp.int32, (blocksize, LANES), 1) < blocksize
    per_part = width // LANES
    for n, part in enumerate(parts):
        for q in range(per_part):
            at = 2 * (part * per_part + q)
            left = pl.multiple_of(codes_smem[r, at] * LANES, LANES)
            right = pl.multiple_of(codes_smem[r, at + 1] * LANES, LANES)
            to = n * width + q * LANES
            spread_ref[c, i * blocksize : (i + 1) * blocksize, to : to + LANES] = jnp.where(
                low_half, tiles_ref[:, pl.ds(left, LANES)], tiles_ref[:, pl.ds(right, LANES)]
            )


def multiply(margin_ref, spread_ref, c, outs):
    depth, total = spread_ref.shape[1:]
    width = total // len(outs)
    step = 256
    for t in range(total // step):
        product = jnp.dot(
            margin_ref[:, c * depth : (c + 1) * depth],
            spread_ref[c, :, t * step : (t + 1) * step],
            preferred_element_type=jnp.float32,
        )
        out = outs[t * step // width]
        at = slice(t * step % width, t * step % width + step)
        out[:, at] = product if c == 0 else out[:, at] + product


def place_and_multiply(
    tiles_ref, spread_ref, codes_smem, codes_copy, margin_ref, copies, parts, outs, prepare
):
    blocksize = tiles_ref.shape[0]
    block_rows = len(copies)
    packed = (tiles_ref.shape[1] - LANES) // (2 * block_rows)
    per_chunk = block_rows // CHUNKS
    width = margin_ref.shape[1]
    tiles_ref[:, tiles_ref.shape[1] - LANES :] = jnp.zeros((blocksize, LANES), jnp.bfloat16)
    for c in range(CHUNKS):
        rows = range(c * per_chunk, (c + 1) * per_chunk)
        for r in rows:
            copies[r].wait()
        for r in rows:
            turn(tiles_ref, r, packed, blocksize)
        if c == 0:
            prepare()
            codes_copy.wait()
        for i, r in enumerate(rows):
            place(tiles_ref, spread_ref, codes_smem, c, i, r, parts, width)
        if c > 0:
            multiply(margin_ref, spread_ref, c - 1, outs)
    multiply(margin_ref, spread_ref, CHUNKS - 1, outs)


def tile_scratch(weights, parts, width):
    block_rows, blocksize, packed = weights.shape
    return [
        pltpu.VMEM((blocksize, block_rows * 2 * packed + LANES), jnp.bfloat16),
        pltpu.VMEM((CHUNKS, block_rows * blocksize // CHUNKS, parts * width), jnp.bfloat16),
    ]


def outgoing(
    total_blocks,
    base_ref,
    labels_hbm,
    cols_hbm,
    scores_hbm,
    weights_hbm,
    down_ref,
    up_ref,
    margin_hbm,
    codes_ref,
    labels_ref,
    cols_ref,
    scores_ref,
    margin_ref,
    tiles_ref,
    spread_ref,
    codes_smem,
    small_sems,
    sems,
):
    cols_copy = pltpu.make_async_copy(cols_hbm, cols_ref, small_sems.at[0])
    labels_copy = pltpu.make_async_copy(labels_hbm, labels_ref, small_sems.at[1])
    scores_copy = pltpu.make_async_copy(scores_hbm, scores_ref, small_sems.at[2])
    cols_copy.start()
    labels_copy.start()
    scores_copy.start()
    copies = start_weights(weights_hbm, tiles_ref, sems)
    classes, samples, width = scores_ref.shape
    cols_copy.wait()
    codes_ref[...] = make_codes(
        cols_ref[...], base_ref[0], total_blocks, weights_hbm.shape[2] // LANES
    )
    codes_copy = pltpu.make_async_copy(codes_ref, codes_smem, small_sems.at[3])
    codes_copy.start()
    margin_copy = pltpu.make_async_copy(margin_ref, margin_hbm, small_sems.at[4])

    def prepare():
        labels_copy.wait()
        row = lax.broadcasted_iota(jnp.int32, (samples, width), 0)
        labels = jnp.zeros((samples, width), jnp.int32)
        for s in range(samples):
            labels = jnp.where(row == s, labels_ref[s], labels)
        scores_copy.wait()
        scores = [scores_ref[c].astype(jnp.float32) for c in range(classes)]
        top = scores[0]
        for c in range(1, classes):
            top = jnp.where(labels == c, scores[c], top)
        for j in range(classes - 1):
            rest = jnp.where(labels > j, scores[j], scores[j + 1])
            margin_ref[pl.ds(j * samples, samples), :] = (top - rest).astype(jnp.bfloat16)
        margin_copy.start()

    place_and_multiply(
        tiles_ref, spread_ref, codes_smem, codes_copy, margin_ref, copies, (0, 2), (down_ref, up_ref), prepare
    )
    margin_copy.wait()


def place_in_run(base_ref, weights_hbm):
    per_dev = weights_hbm.shape[0]
    return lax.rem(lax.div(base_ref[0] + per_dev, jnp.int32(per_dev)), jnp.int32(RUN))


def first_kernel(total_blocks, base_ref, *refs):
    @pl.when(place_in_run(base_ref, refs[3]) != RUN - 1)
    def _():
        outgoing(total_blocks, base_ref, *refs)


def late_kernel(
    total_blocks,
    base_ref,
    labels_hbm,
    cols_hbm,
    scores_hbm,
    weights_hbm,
    early_down_ref,
    early_margin_hbm,
    early_codes_ref,
    down_ref,
    margin_hbm,
    codes_ref,
    outer_ref,
    *scratch,
):
    del early_margin_hbm, early_codes_ref
    index = place_in_run(base_ref, weights_hbm)

    @pl.when(index == RUN - 1)
    def _():
        outgoing(
            total_blocks,
            base_ref,
            labels_hbm,
            cols_hbm,
            scores_hbm,
            weights_hbm,
            down_ref,
            outer_ref,
            margin_hbm,
            codes_ref,
            *scratch,
        )

    @pl.when(index == 0)
    def _():
        outer_ref[...] = early_down_ref[...]


def late(total_blocks, base, labels, cols, scores, weights, down, margin, codes):
    rows, width = down.shape
    samples = labels.shape[0]
    block_rows = weights.shape[0]
    hbm = pl.BlockSpec(memory_space=pltpu.HBM)
    vmem = pl.BlockSpec(memory_space=pltpu.VMEM)
    return pl.pallas_call(
        functools.partial(late_kernel, total_blocks),
        out_shape=(
            pltpu.VMEM((rows, width), jnp.float32),
            jax.ShapeDtypeStruct((rows, width), jnp.bfloat16),
            pltpu.VMEM((block_rows, LANES), jnp.int32),
            pltpu.VMEM((rows, width), jnp.float32),
        ),
        in_specs=[pl.BlockSpec(memory_space=pltpu.SMEM), hbm, hbm, hbm, hbm, vmem, hbm, vmem],
        out_specs=(vmem, hbm, vmem, vmem),
        input_output_aliases={5: 0, 6: 1, 7: 2},
        scratch_shapes=[
            pltpu.SMEM((samples,), jnp.int32),
            pltpu.VMEM(cols.shape, jnp.int32),
            pltpu.VMEM(scores.shape, jnp.bfloat16),
            pltpu.VMEM((rows, width), jnp.bfloat16),
            *tile_scratch(weights, 2, width),
            pltpu.SMEM((block_rows, LANES), jnp.int32),
            pltpu.SemaphoreType.DMA((5,)),
            pltpu.SemaphoreType.DMA((block_rows,)),
        ],
        compiler_params=pltpu.CompilerParams(vmem_limit_bytes=59 << 20),
        cost_estimate=pl.CostEstimate(
            flops=4 * rows * width * width, bytes_accessed=6 << 20, transcendentals=0
        ),
        name="late",
    )(base, labels, cols, scores, weights, down, margin, codes)


def first(total_blocks, base, labels, cols, scores, weights):
    classes, samples, width = scores.shape
    rows = (classes - 1) * samples
    block_rows = weights.shape[0]
    hbm = pl.BlockSpec(memory_space=pltpu.HBM)
    vmem = pl.BlockSpec(memory_space=pltpu.VMEM)
    return pl.pallas_call(
        functools.partial(first_kernel, total_blocks),
        out_shape=(
            pltpu.VMEM((rows, width), jnp.float32),
            pltpu.VMEM((rows, width), jnp.float32),
            jax.ShapeDtypeStruct((rows, width), jnp.bfloat16),
            pltpu.VMEM((block_rows, LANES), jnp.int32),
        ),
        in_specs=[pl.BlockSpec(memory_space=pltpu.SMEM), hbm, hbm, hbm, hbm],
        out_specs=(vmem, vmem, hbm, vmem),
        scratch_shapes=[
            pltpu.SMEM((samples,), jnp.int32),
            pltpu.VMEM(cols.shape, jnp.int32),
            pltpu.VMEM(scores.shape, jnp.bfloat16),
            pltpu.VMEM((rows, width), jnp.bfloat16),
            *tile_scratch(weights, 2, width),
            pltpu.SMEM((block_rows, LANES), jnp.int32),
            pltpu.SemaphoreType.DMA((5,)),
            pltpu.SemaphoreType.DMA((block_rows,)),
        ],
        compiler_params=pltpu.CompilerParams(vmem_limit_bytes=60 << 20),
        cost_estimate=pl.CostEstimate(
            flops=4 * rows * width * width, bytes_accessed=6 << 20, transcendentals=0
        ),
        name="first",
    )(base, labels, cols, scores, weights)


def second_kernel(
    flags_ref,
    codes_vmem,
    bias_ref,
    mid_ref,
    rad_ref,
    slope_ref,
    margin_hbm,
    weights_hbm,
    centre_ref,
    bias_acc_ref,
    slopes_ref,
    margin_ref,
    tiles_ref,
    spread_ref,
    codes_smem,
    small_sems,
    sems,
):
    codes_copy = pltpu.make_async_copy(codes_vmem, codes_smem, small_sems.at[0])
    codes_copy.start()
    margin_copy = pltpu.make_async_copy(margin_hbm, margin_ref, small_sems.at[1])
    margin_copy.start()
    copies = start_weights(weights_hbm, tiles_ref, sems)
    width = margin_ref.shape[1]
    margin_copy.wait()
    terms = margin_ref[...].astype(jnp.float32) * bias_ref[...]
    acc = terms[:, :LANES]
    for t in range(1, width // LANES):
        acc = acc + terms[:, t * LANES : (t + 1) * LANES]
    bias_acc_ref[...] = acc
    lower = mid_ref[...] - rad_ref[...]
    upper = mid_ref[...] + rad_ref[...]
    up_slope = (jnp.maximum(upper, 0.0) - jnp.maximum(lower, 0.0)) / (upper - lower)
    blocks = flags_ref.shape[0]
    block = lax.broadcasted_iota(jnp.int32, (1, width), 1) // (width // blocks)
    flags = jnp.zeros((1, width), jnp.int32)
    for b in range(blocks):
        flags = jnp.where(block == b, flags_ref[b], flags)
    slopes_ref[0:1] = jnp.where(flags == 1, slope_ref[...], up_slope)
    slopes_ref[1:2] = up_slope
    slopes_ref[2:3] = jnp.maximum(lower, 0.0) - up_slope * lower
    place_and_multiply(
        tiles_ref, spread_ref, codes_smem, codes_copy, margin_ref, copies, (1,), (centre_ref,), lambda: None
    )


def second(flags, codes, bias, mid, rad, slope, margin, weights):
    rows, width = margin.shape
    block_rows = weights.shape[0]
    vmem = pl.BlockSpec(memory_space=pltpu.VMEM)
    return pl.pallas_call(
        second_kernel,
        out_shape=(
            pltpu.VMEM((rows, width), jnp.float32),
            pltpu.VMEM((rows, LANES), jnp.float32),
            pltpu.VMEM((3, width), jnp.float32),
        ),
        in_specs=[pl.BlockSpec(memory_space=pltpu.SMEM)]
        + [vmem] * 5
        + [pl.BlockSpec(memory_space=pltpu.HBM)] * 2,
        out_specs=(vmem, vmem, vmem),
        scratch_shapes=[
            pltpu.VMEM((rows, width), jnp.bfloat16),
            *tile_scratch(weights, 1, width),
            pltpu.SMEM((block_rows, LANES), jnp.int32),
            pltpu.SemaphoreType.DMA((2,)),
            pltpu.SemaphoreType.DMA((block_rows,)),
        ],
        compiler_params=pltpu.CompilerParams(vmem_limit_bytes=30 << 20),
        cost_estimate=pl.CostEstimate(
            flops=2 * rows * width * width, bytes_accessed=6 << 20, transcendentals=0
        ),
        name="second",
    )(flags, codes, bias, mid, rad, slope, margin, weights)


def sums_kernel(slopes_ref, bias_acc_ref, centre_ref, higher_ref, lower_ref, closing_ref, offs_ref, acc_ref):
    rows, width = centre_ref.shape
    up_shift = slopes_ref[2:3]
    part = 24
    for first_row in range(0, rows, part):
        at = slice(first_row, first_row + part)
        propagated = centre_ref[at] + higher_ref[at] + lower_ref[at] + closing_ref[at]
        terms = jnp.minimum(propagated, 0.0) * up_shift
        acc = bias_acc_ref[at]
        for t in range(width // LANES):
            acc = acc + terms[:, t * LANES : (t + 1) * LANES]
        acc_ref[at] = acc
    sums = lax.dot_general(
        jnp.ones((8, LANES), jnp.float32),
        acc_ref[...],
        (((1,), (1,)), ((), ())),
        precision=lax.Precision.HIGHEST,
        preferred_element_type=jnp.float32,
    )
    for d in range(offs_ref.shape[0]):
        offs_ref[d] = sums[:1]


def sums(devices, slopes, bias_acc, centre, higher, lower, closing):
    rows, _ = centre.shape
    vmem = pl.BlockSpec(memory_space=pltpu.VMEM)
    return pl.pallas_call(
        sums_kernel,
        out_shape=pltpu.VMEM((devices, 1, rows), jnp.float32),
        in_specs=[vmem] * 6,
        out_specs=vmem,
        scratch_shapes=[pltpu.VMEM((rows, LANES), jnp.float32)],
        compiler_params=pltpu.CompilerParams(vmem_limit_bytes=16 << 20),
        name="sums",
    )(slopes, bias_acc, centre, higher, lower, closing)


def last_kernel(
    slopes_ref,
    centre_ref,
    higher_ref,
    lower_ref,
    closing_ref,
    gathered_ref,
    coef_hbm,
    out_hbm,
    coef_ref,
    out_ref,
    coef_sems,
    out_sem,
):
    specs, samples, _ = coef_ref.shape
    total = gathered_ref[0]
    for d in range(1, gathered_ref.shape[0]):
        total = total + gathered_ref[d]
    for j in range(specs):
        out_ref[j : j + 1, :] = total[:, j * samples : (j + 1) * samples]
    copies = [pltpu.make_async_copy(out_ref, out_hbm, out_sem)]
    copies[0].start()
    low_slope = slopes_ref[0:1]
    up_slope = slopes_ref[1:2]
    for j in range(specs):
        at = slice(j * samples, (j + 1) * samples)
        propagated = centre_ref[at] + higher_ref[at] + lower_ref[at] + closing_ref[at]
        positive = jnp.maximum(propagated, 0.0)
        negative = jnp.minimum(propagated, 0.0)
        coef_ref[j] = (low_slope * positive + up_slope * negative).astype(jnp.bfloat16)
        copies.append(pltpu.make_async_copy(coef_ref.at[j], coef_hbm.at[j], coef_sems.at[j]))
        copies[-1].start()
    for copy in copies:
        copy.wait()


def last(samples, slopes, centre, higher, lower, closing, gathered):
    rows, width = centre.shape
    specs = rows // samples
    vmem = pl.BlockSpec(memory_space=pltpu.VMEM)
    hbm = pl.BlockSpec(memory_space=pltpu.HBM)
    return pl.pallas_call(
        last_kernel,
        out_shape=(
            jax.ShapeDtypeStruct((specs, samples, width), jnp.bfloat16),
            jax.ShapeDtypeStruct((specs, samples), jnp.float32),
        ),
        in_specs=[vmem] * 6,
        out_specs=(hbm, hbm),
        scratch_shapes=[
            pltpu.VMEM((specs, samples, width), jnp.bfloat16),
            pltpu.VMEM((specs, samples), jnp.float32),
            pltpu.SemaphoreType.DMA((specs,)),
            pltpu.SemaphoreType.DMA,
        ],
        compiler_params=pltpu.CompilerParams(vmem_limit_bytes=16 << 20),
        name="last",
    )(slopes, centre, higher, lower, closing, gathered)


def local(
    class_scores,
    true_class,
    weight_blocks,
    col_blocks,
    layer_bias,
    bound_mid,
    bound_rad,
    lower_slope,
    unstable_blocks,
):
    samples, _, width = class_scores.shape
    per_dev = col_blocks.shape[0]
    devices = lax.axis_size("neuron")
    position = lax.axis_index("neuron")
    base = ((position - 1) * per_dev).astype(jnp.int32).reshape(1)
    scores = jnp.transpose(class_scores, (1, 0, 2))
    total_blocks = devices * per_dev
    down, up, margin, codes = first(
        total_blocks, base, true_class, col_blocks, scores, weight_blocks
    )
    starts = range(0, devices, RUN)
    ends = range(RUN - 1, devices, RUN)
    lower = send(up, [(i, i + 1) for i in range(devices) if i not in ends])
    down, margin, codes, outer = late(
        total_blocks, base, true_class, col_blocks, scores, weight_blocks, down, margin, codes
    )
    higher = send(down, [(i, i - 1) for i in range(devices) if i not in starts])
    closing = send(
        outer,
        [(i, (i - 1) % devices) for i in starts] + [(i, (i + 1) % devices) for i in ends],
    )
    bias = layer_bias.astype(jnp.float32).reshape(1, width)
    centre, bias_acc, slopes = second(
        unstable_blocks,
        codes,
        bias,
        bound_mid.reshape(1, width),
        bound_rad.reshape(1, width),
        lower_slope.reshape(1, width),
        margin,
        weight_blocks,
    )
    offs = sums(devices, slopes, bias_acc, centre, higher, lower, closing)
    gathered = lax.all_to_all(offs, "neuron", 0, 0)
    coef, offsets = last(samples, slopes, centre, higher, lower, closing, gathered)
    return jnp.transpose(coef, (1, 0, 2)), offsets.T


def solution(mesh):
    placed = (
        P("spec", None, "neuron"),
        P("spec"),
        P("neuron", None, None),
        P("neuron", None),
        P("neuron"),
        P("neuron"),
        P("neuron"),
        P("neuron"),
        P("neuron"),
    )
    return jax.shard_map(
        local,
        mesh=mesh,
        in_specs=placed,
        out_specs=(P("spec", None, "neuron"), P("spec", None)),
        check_vma=False,
    )
```
